512 devices in a mesh: fsdp: 64 (over y, z_lo, core), ctx: 8 (over x, z_hi).
Axes of the slice: x: 4, y: 8, z: 8 (z_hi: 2, z_lo: 4; z = z_hi * 4 + z_lo), core: 2. Of those that a mesh axis runs over, the one named last changes fastest.
Arguments:
- activations: bfloat16 [4096, 5120], P('fsdp', 'ctx'), may hold values from -500 to 500
- norm_gain: float32 [4096], P('fsdp'), may hold values from 0.25 to 1.75
- w_in: bfloat16 [3, 4096, 4096], P(None, 'fsdp'), may hold values from -0.09375 to 0.09375
- w_short: float32 [3, 4096, 3], P(None, 'fsdp'), may hold values from -3.5 to 3.5
- long_filter: bfloat16 [4096, 5120], P('fsdp'), may hold values from -1.1 to 1.1
- skip_gain: float32 [4096], P('fsdp'), may hold values from -4 to 4
- w_out: bfloat16 [4096, 4096], P('fsdp'), may hold values from -0.09375 to 0.09375
Outputs:
- mixer_out: bfloat16 [4096, 5120], P('fsdp', 'ctx')
The draws below stay inside these ranges and needn't reach their ends.
All inputs are finite; a program needn't handle non-finite values.
Results may differ from the reference program's by a relative error of at most 0.035.
Values may be sent and summed in bfloat16 or wider, within the bound.
A program may use at most 64 MiB of HBM per device.

```python
import jax
import jax.numpy as jnp
from jax import lax

CHANNEL_COUNT = 4096
SHORT = 3
GENOME_LETTERS = 5120


def draw_activations(key, part):
    stochastic_seed_parts = jax.random.split(key, 3)
    row_pos = jnp.arange(CHANNEL_COUNT, dtype=jnp.float32) / max(CHANNEL_COUNT - 1, 1)
    rising = jnp.exp(jnp.log(3.0) * row_pos)
    random_part = jax.random.truncated_normal(stochastic_seed_parts[0], -4.0, 4.0, (CHANNEL_COUNT, GENOME_LETTERS), jnp.float32)
    feature_scale = jnp.exp(jax.random.uniform(stochastic_seed_parts[1], (CHANNEL_COUNT,), jnp.float32, 0.0, jnp.log(10.0)))
    token_scale = jnp.exp(jax.random.uniform(stochastic_seed_parts[2], (GENOME_LETTERS,), jnp.float32, 0.0, jnp.log(10.0)))
    return (random_part * (rising * feature_scale)[:, None] * token_scale[None, :] * 0.25).astype(jnp.bfloat16)


def draw_long_filter(key, part):
    stochastic_seed_parts = jax.random.split(key, 6)
    quick_share = 0.35
    quick_mask = jax.random.bernoulli(stochastic_seed_parts[0], quick_share, (CHANNEL_COUNT,))
    quick_rate = 1.0 / jax.random.uniform(stochastic_seed_parts[1], (CHANNEL_COUNT,), jnp.float32, 30.0, 50.0)
    slow_rate = jnp.exp(jax.random.uniform(stochastic_seed_parts[2], (CHANNEL_COUNT,), jnp.float32, jnp.log(0.2), jnp.log(2.0))) / GENOME_LETTERS
    decay_rate = jnp.where(quick_mask, quick_rate, slow_rate)
    delay_offset_number = jnp.arange(GENOME_LETTERS, dtype=jnp.float32)
    kernel_decay_profile = jnp.exp(-decay_rate[:, None] * delay_offset_number[None, :])
    spike_offset = jax.random.randint(stochastic_seed_parts[3], (CHANNEL_COUNT, 3), 1, GENOME_LETTERS).astype(jnp.float32)
    spike_survives = jax.random.uniform(stochastic_seed_parts[4], (CHANNEL_COUNT, 3), jnp.float32, 0.5, 0.8)
    for spike_segment_number in range(3):
        completed_segments = delay_offset_number[None, :] >= spike_offset[:, spike_segment_number][:, None]
        kernel_decay_profile = kernel_decay_profile * jnp.where(completed_segments, spike_survives[:, spike_segment_number][:, None], 1.0)
    amplitude = jnp.sqrt(2.0 * decay_rate / (1.0 - jnp.exp(-2.0 * decay_rate * GENOME_LETTERS)))
    random_part = jax.random.truncated_normal(stochastic_seed_parts[5], -4.0, 4.0, (CHANNEL_COUNT, GENOME_LETTERS), jnp.float32)
    return (amplitude[:, None] * kernel_decay_profile * random_part).astype(jnp.bfloat16)


def block_levels(own_key, shape, cuts, low, high):
    factor_of, own = 1.0, jax.random.fold_in(own_key, 6)
    for dim, shards_of in cuts:
        draws = jnp.exp(jax.random.uniform(jax.random.fold_in(own, dim), (shards_of,), jnp.float32, low / len(cuts), high / len(cuts)))
        factor_of = factor_of * jnp.repeat(draws, shape[dim] // shards_of).reshape([-1 if axis == dim else 1 for axis in range(len(shape))])
    return factor_of


def centred(stream_key, shape, width, limit, pieces=(), held_as=jnp.bfloat16):
    factor_of = block_levels(stream_key, shape, pieces, -0.22, 0.18) if pieces else 1.0
    result = jax.random.normal(stream_key, shape, jnp.float32) * width * factor_of
    return jnp.minimum(jnp.maximum(result, -limit), limit).astype(held_as)


def setup_inputs(seed: int = 0) -> dict:
    streams_of = jax.random.split(jax.random.key(seed), 8)
    activations = draw_activations(jax.random.fold_in(streams_of[7], 71), 0)
    norm_gain = jnp.clip(1.0 + 0.15 * jax.random.normal(streams_of[1], (CHANNEL_COUNT,), jnp.float32), 0.25, 1.75)
    w_in = centred(streams_of[2], (3, CHANNEL_COUNT, CHANNEL_COUNT), CHANNEL_COUNT ** -0.5, 0.09375, ((1, 64),))
    w_short = centred(streams_of[3], (3, CHANNEL_COUNT, SHORT), SHORT ** -0.5, 3.5, ((1, 64),), jnp.float32)
    long_filter = draw_long_filter(jax.random.fold_in(streams_of[7], 71), 0)
    skip_gain = centred(streams_of[5], (CHANNEL_COUNT,), 1.0, 4.0, ((0, 64),), jnp.float32)
    w_out = centred(streams_of[6], (CHANNEL_COUNT, CHANNEL_COUNT), CHANNEL_COUNT ** -0.5, 0.09375, ((0, 64),))
    return {"activations": activations, "norm_gain": norm_gain, "w_in": w_in, "w_short": w_short, "long_filter": long_filter, "skip_gain": skip_gain, "w_out": w_out}


epsilon = 1e-05

def reference(activations, norm_gain, w_in, w_short, long_filter, skip_gain, w_out):
    wide = activations.astype(jnp.float32)
    factor = lax.rsqrt(lax.optimization_barrier(jnp.mean(wide * wide, axis=0)) + epsilon)
    normed = (wide * factor[None, :] * norm_gain[:, None]).astype(jnp.bfloat16)
    projected = jnp.stack([jnp.dot(w_in[stream], normed, preferred_element_type=jnp.float32) for stream in range(3)]).astype(jnp.bfloat16)
    padded = jnp.pad(projected.astype(jnp.float32), ((0, 0), (0, 0), (SHORT - 1, 0)))
    smoothed = jnp.zeros(projected.shape, jnp.float32)
    for tap_index in range(SHORT):
        begin = SHORT - 1 - tap_index
        smoothed = smoothed + w_short[:, :, tap_index][:, :, None] * padded[:, :, begin:begin + GENOME_LETTERS]
    query = smoothed[0]
    key_part = smoothed[1]
    value = smoothed[2]
    gated = (key_part * value).astype(jnp.bfloat16)
    expanded = long_filter.astype(jnp.float32)
    length = 2 * GENOME_LETTERS
    spectrum = jnp.fft.rfft(gated.astype(jnp.float32), n=length, axis=1) * jnp.fft.rfft(expanded, n=length, axis=1)
    filtered = jnp.fft.irfft(spectrum, n=length, axis=1)[:, :GENOME_LETTERS]
    mixed = (query * (filtered + skip_gain[:, None] * gated.astype(jnp.float32))).astype(jnp.bfloat16)
    return jnp.dot(w_out, mixed, preferred_element_type=jnp.float32).astype(jnp.bfloat16)
```

```python
import functools

import jax
import jax.numpy as jnp
from jax import lax
from jax.experimental import pallas as pl
from jax.experimental.pallas import tpu as pltpu
from jax.sharding import PartitionSpec as P

EPSILON = 1e-05
MESH = pl.DeviceIdType.MESH
LANES = 128
ROWS = 8


class Plan:
    def __init__(self, fsdp, ctx, rows, tokens, long_len):
        self.cores = 2
        self.ring = {64: 8, 16: 4, 8: 4}[fsdp]
        self.line = fsdp // (self.ring * self.cores)
        self.plane = self.line * self.cores
        self.fsdp, self.ctx = fsdp, ctx
        self.rows, self.tokens, self.long_len = rows, tokens, long_len
        self.half = self.ring // 2
        self.blocks = long_len // LANES
        self.token_tiles = tokens // LANES


def copy_to(src, dst, send, recv, device):
    return pltpu.make_async_remote_copy(
        src_ref=src, dst_ref=dst, send_sem=send, recv_sem=recv, device_id=device, device_id_type=MESH
    )


def kernel(
    plan, act, gain, w_in, w_short, filt, skip, w_out, out,
    gath, mixg, win, wout, xin, hin, hrow, tmat, acc, acc2, plane_sum, ring_sum,
    pbuf, rbuf, mbuf, mrecv, seq, gseq, fseq, skipb,
    lsem, plane_sem, ring_sem, zsem, ysem, csem, zsem2, ysem2, csem2, asem, bsem,
):
    me = lax.axis_index("fsdp")
    ctx = lax.axis_index("ctx")
    ring, line, plane, half = plan.ring, plan.line, plan.plane, plan.half
    y = me // plane
    p = lax.rem(me, plane)
    z = p // plan.cores
    core = lax.rem(p, plan.cores)
    rows, tokens = plan.rows, plan.tokens

    def at(yy, zz, cc):
        return (yy * line + zz) * plan.cores + cc

    def turn(yy):
        return lax.rem(yy + 2 * ring, ring)

    loads = [
        pltpu.make_async_copy(act, xin, lsem.at[0]),
        pltpu.make_async_copy(filt.at[ctx], hin, lsem.at[1]),
        pltpu.make_async_copy(w_in, win, lsem.at[2]),
        pltpu.make_async_copy(w_out, wout, lsem.at[3]),
    ]
    for load in loads:
        load.start()

    barrier = pltpu.get_barrier_semaphore()

    def greet(device):
        pl.semaphore_signal(barrier, inc=1, device_id=device, device_id_type=MESH)

    @pl.loop(1, plane)
    def _(o):
        greet({"fsdp": y * plane + (p ^ o)})

    @pl.loop(1, ring)
    def _(o):
        greet({"fsdp": turn(y + o) * plane + p})

    if plan.ctx > 1:
        @pl.loop(1, plan.ctx)
        def _(o):
            greet({"ctx": ctx ^ o})

    def column(row):
        n = row.shape[1]
        same = lax.broadcasted_iota(jnp.int32, (n, n), 0) == lax.broadcasted_iota(jnp.int32, (n, n), 1)
        return jnp.sum(jnp.where(same, jnp.broadcast_to(row, (n, n)), 0.0), axis=1, keepdims=True)

    loads[0].wait()
    own = xin[...].astype(jnp.float32)
    gath[me] = (own * column(gain[...])).astype(jnp.bfloat16)
    squares = jnp.sum(own * own, axis=0, keepdims=True)
    plane_sum[0] = jnp.zeros((ROWS, LANES), jnp.float32)
    for k in range(plan.token_tiles):
        plane_sum[0, k : k + 1, :] = squares[:, k * LANES : (k + 1) * LANES]
    skipb[...] = jnp.broadcast_to(column(skip[...]), (rows, LANES))
    acc[...] = jnp.zeros_like(acc)
    acc2[...] = jnp.zeros_like(acc2)
    gseq[...] = jnp.zeros_like(gseq)
    seq[:, :, :LANES] = jnp.zeros((3, ROWS, LANES), jnp.float32)
    pl.semaphore_wait(barrier, (plane - 1) + (ring - 1) + (plan.ctx - 1))

    def plane_copy(o):
        return copy_to(
            plane_sum.at[0], plane_sum.at[o], plane_sem.at[0, o], plane_sem.at[1, o], {"fsdp": y * plane + (p ^ o)}
        )

    def ring_copy(o):
        return copy_to(
            ring_sum.at[0], ring_sum.at[o], ring_sem.at[0, o], ring_sem.at[1, o], {"fsdp": turn(y + o) * plane + p}
        )

    def gather(buf, zs, ys, cs, multiply, fillers):
        def zcopy(o, zz_from):
            block = buf.at[at(y, zz_from, core)]
            return copy_to(block, block, zs.at[0, o], zs.at[1, o], {"fsdp": at(y, z ^ o, core)})

        def origin(d, s):
            return turn(y - s) if d == 0 else turn(y + s)

        def part(block, d, s):
            if s < half:
                return buf.at[block]
            return buf.at[block, pl.ds(d * (rows // 2), rows // 2)]

        def ycopy(d, s, o, receive):
            came = s if receive else s - 1
            block = at(origin(d, came), z ^ o, core)
            view = part(block, d, s)
            to = turn(y + 1) if d == 0 else turn(y - 1)
            return copy_to(view, view, ys.at[0, d, s - 1, o], ys.at[1, d, s - 1, o], {"fsdp": at(to, z, core)})

        def ccopy(d, s, o, mine):
            r = s + d * half
            block = at(origin(d, s), z ^ o, core if mine else 1 - core)
            view = part(block, d, s)
            return copy_to(view, view, cs.at[0, r, o], cs.at[1, r, o], {"fsdp": at(y, z, 1 - core)})

        for o in range(1, line):
            zcopy(o, z).start()
        for d in range(2):
            ycopy(d, 1, 0, False).start()
        ccopy(0, 0, 0, True).start()
        fillers[0]()
        for o in range(1, line):
            zcopy(o, z ^ o).wait_recv()
            for d in range(2):
                ycopy(d, 1, o, False).start()
            ccopy(0, 0, o, True).start()
        fillers[1]()
        for s in range(1, half + 1):
            @pl.loop(0, line)
            def _(o):
                for d in range(2):
                    ycopy(d, s, o, True).wait_recv()
                    if s < half:
                        ycopy(d, s + 1, o, False).start()
                    ccopy(d, s, o, True).start()

            @pl.loop(0, line)
            def _(o):
                for d in range(2 if s > 1 else 1):
                    ccopy(d, s - 1, o, False).wait_recv()

            for d in range(2 if s > 1 else 1):
                multiply(origin(d, s - 1))
            fillers[1 + s]()

        @pl.loop(0, line)
        def _(o):
            for d in range(2):
                ccopy(d, half, o, False).wait_recv()

        multiply(origin(0, half))

        def drain():
            for o in range(1, line):
                zcopy(o, z).wait_send()

            @pl.loop(0, line)
            def _(o):
                ccopy(0, 0, o, True).wait_send()
                for s in range(1, half + 1):
                    for d in range(2):
                        ycopy(d, s, o, False).wait_send()
                        ccopy(d, s, o, True).wait_send()

        return drain

    width = plane * rows

    def multiply_in(yy):
        w = win[:, :, pl.ds(pl.multiple_of(yy * width, width), width)].reshape(3 * rows, width)
        x = gath[pl.ds(yy * plane, plane)].reshape(width, tokens)
        acc[...] += jnp.dot(w, x, preferred_element_type=jnp.float32)

    def multiply_out(yy):
        w = wout[:, pl.ds(pl.multiple_of(yy * width, width), width)]
        x = mixg[pl.ds(yy * plane, plane)].reshape(width, tokens)
        acc2[...] += jnp.dot(w, x, preferred_element_type=jnp.float32)

    def spread_filter():
        for load in loads[1:]:
            load.wait()
        h = hin[...].astype(jnp.float32)
        for d in range(plan.blocks):
            hrow[pl.ds(d, ROWS, stride=plan.blocks), :] = h[:, d * LANES : (d + 1) * LANES]

    later = lax.broadcasted_iota(jnp.int32, (LANES, LANES), 1) >= lax.broadcasted_iota(jnp.int32, (LANES, LANES), 0)

    def band(first, last):
        @pl.loop(first, last)
        def _(c):
            def body(d, before):
                r = c * plan.blocks + d
                line_ = jnp.broadcast_to(hrow[pl.ds(r, 1), :], (LANES, LANES))
                rolled = pltpu.roll(line_, 0, 1, stride=1, stride_axis=0)
                tmat[r] = jnp.where(later, rolled, before).astype(jnp.bfloat16)
                return rolled

            lax.fori_loop(0, plan.blocks, body, jnp.zeros((LANES, LANES), jnp.float32))

    def start_plane():
        @pl.loop(1, plane)
        def _(o):
            plane_copy(o).start()

        spread_filter()

    def start_ring():
        @pl.loop(1, plane)
        def _(o):
            plane_copy(o).wait_recv()

        ring_sum[0] = jnp.sum(plane_sum[...], axis=0)

        @pl.loop(1, ring)
        def _(o):
            ring_copy(o).start()

        band(0, 2)

    bands = [functools.partial(band, 2 + 6 * i // half, 2 + 6 * (i + 1) // half) for i in range(half)]
    drain1 = gather(gath, zsem, ysem, csem, multiply_in, [start_plane, start_ring] + bands)

    @pl.loop(1, ring)
    def _(o):
        ring_copy(o).wait_recv()

    features = plan.fsdp * rows
    factor = lax.rsqrt(jnp.sum(ring_sum[...], axis=0) / features + EPSILON)
    for k in range(plan.token_tiles):
        lanes = slice(k * LANES, (k + 1) * LANES)
        for s in range(3):
            scaled = acc[s * rows : (s + 1) * rows, lanes] * factor[k : k + 1, :]
            for j in range(plan.ctx):
                n = rows // plan.ctx
                pbuf[j, s, :, lanes] = scaled[j * n : (j + 1) * n].astype(jnp.bfloat16)

    def swap(src, dst, sem):
        def one(o):
            return copy_to(src.at[ctx ^ o], dst.at[ctx], sem.at[0, o], sem.at[1, o], {"ctx": ctx ^ o})

        def arrival(o):
            return copy_to(src.at[ctx ^ o], dst.at[ctx ^ o], sem.at[0, o], sem.at[1, o], {"ctx": ctx ^ o})

        if plan.ctx > 1:
            @pl.loop(1, plan.ctx)
            def _(o):
                one(o).start()

        dst[ctx] = src[ctx]
        if plan.ctx > 1:
            @pl.loop(1, plan.ctx)
            def _(o):
                arrival(o).wait_recv()

        def drain():
            if plan.ctx > 1:
                @pl.loop(1, plan.ctx)
                def _(o):
                    one(o).wait_send()

        return drain

    drain2 = swap(pbuf, rbuf, asem)

    for j in range(plan.ctx):
        for s in range(3):
            seq[s, :, LANES + j * tokens : LANES + (j + 1) * tokens] = rbuf[j, s].astype(jnp.float32)

    def smooth(s):
        taps = w_short[s, ctx]
        full = seq[s]
        total = taps[:, 0:1] * full + taps[:, 1:2] * pltpu.roll(full, 1, 1)
        total = total + taps[:, 2:3] * pltpu.roll(full, 2, 1)
        return total[:, LANES:]

    gated = (smooth(1) * smooth(2)).astype(jnp.bfloat16).astype(jnp.float32)
    query = smooth(0)
    blocks = plan.blocks
    for b in range(blocks):
        gseq[pl.ds(blocks + b, ROWS, stride=2 * blocks), :] = gated[:, b * LANES : (b + 1) * LANES]

    @pl.loop(0, ROWS)
    def _(c):
        base = c * 2 * blocks + blocks
        lhs = jnp.concatenate(
            [gseq[pl.ds(base - d, blocks), :].astype(jnp.bfloat16) for d in range(blocks)], axis=1
        )
        rhs = tmat[pl.ds(c * blocks, blocks)].reshape(blocks * LANES, LANES)
        fseq[pl.ds(c * blocks, blocks), :] = jnp.dot(lhs, rhs, preferred_element_type=jnp.float32)

    direct = skipb[pl.ds(ctx * ROWS, ROWS), :]
    for b in range(blocks):
        lanes = slice(b * LANES, (b + 1) * LANES)
        value = query[:, lanes] * (fseq[pl.ds(b, ROWS, stride=blocks), :] + direct * gated[:, lanes])
        j, k = b // plan.token_tiles, b % plan.token_tiles
        mbuf[j, :, k * LANES : (k + 1) * LANES] = value.astype(jnp.bfloat16)

    drain3 = swap(mbuf, mrecv, bsem)
    mixg[me] = mrecv[...].astype(jnp.float32).reshape(rows, tokens).astype(jnp.bfloat16)

    nothing = [lambda: None] * (half + 2)
    drain4 = gather(mixg, zsem2, ysem2, csem2, multiply_out, nothing)
    out[...] = acc2[...].astype(jnp.bfloat16)

    @pl.loop(1, plane)
    def _(o):
        plane_copy(o).wait_send()

    @pl.loop(1, ring)
    def _(o):
        ring_copy(o).wait_send()

    drain1()
    drain2()
    drain3()
    drain4()


def shards(fsdp, ctx, activations, norm_gain, w_in, w_short, long_filter, skip_gain, w_out):
    rows, tokens = activations.shape
    long_len = long_filter.shape[1]
    plan = Plan(fsdp, ctx, rows, tokens, long_len)
    groups = rows // ROWS
    features = fsdp * rows
    bf16, f32 = jnp.bfloat16, jnp.float32
    dma = pltpu.SemaphoreType.DMA
    anywhere = pl.BlockSpec(memory_space=pl.ANY)
    here = pl.BlockSpec(memory_space=pltpu.VMEM)
    gather_sems = [
        dma((2, max(plan.line, 2))),
        dma((2, 2, plan.half, plan.line)),
        dma((2, 2 * plan.half + 1, plan.line)),
    ]
    scratch = [
        pltpu.VMEM((fsdp, rows, tokens), bf16),
        pltpu.VMEM((fsdp, rows, tokens), bf16),
        pltpu.VMEM((3, rows, features), bf16),
        pltpu.VMEM((rows, features), bf16),
        pltpu.VMEM((rows, tokens), bf16),
        pltpu.VMEM((ROWS, long_len), bf16),
        pltpu.VMEM((ROWS * plan.blocks, LANES), f32),
        pltpu.VMEM((ROWS * plan.blocks, LANES, LANES), bf16),
        pltpu.VMEM((3 * rows, tokens), f32),
        pltpu.VMEM((rows, tokens), f32),
        pltpu.VMEM((plan.plane, ROWS, LANES), f32),
        pltpu.VMEM((plan.ring, ROWS, LANES), f32),
        pltpu.VMEM((ctx, 3, ROWS, tokens), bf16),
        pltpu.VMEM((ctx, 3, ROWS, tokens), bf16),
        pltpu.VMEM((ctx, ROWS, tokens), bf16),
        pltpu.VMEM((ctx, ROWS, tokens), bf16),
        pltpu.VMEM((3, ROWS, LANES + long_len), f32),
        pltpu.VMEM((ROWS * 2 * plan.blocks, LANES), f32),
        pltpu.VMEM((ROWS * plan.blocks, LANES), f32),
        pltpu.VMEM((rows, LANES), f32),
        dma((4,)),
        dma((2, plan.plane)),
        dma((2, plan.ring)),
        *gather_sems,
        *gather_sems,
        dma((2, ctx)),
        dma((2, ctx)),
    ]
    return pl.pallas_call(
        functools.partial(kernel, plan),
        out_shape=jax.ShapeDtypeStruct((rows, tokens), bf16),
        in_specs=[anywhere, here, anywhere, here, anywhere, here, anywhere],
        out_specs=here,
        scratch_shapes=scratch,
        compiler_params=pltpu.CompilerParams(
            collective_id=0, has_side_effects=True, vmem_limit_bytes=56 * 1024 * 1024
        ),
        name="mixer",
    )(
        activations,
        norm_gain.reshape(1, rows),
        w_in,
        w_short.reshape(3, groups, ROWS, w_short.shape[2]),
        long_filter.reshape(groups, ROWS, long_len),
        skip_gain.reshape(1, rows),
        w_out,
    )


def solution(mesh):
    placed = (
        P("fsdp", "ctx"),
        P("fsdp"),
        P(None, "fsdp", None),
        P(None, "fsdp", None),
        P("fsdp", None),
        P("fsdp"),
        P("fsdp", None),
    )
    body = functools.partial(shards, mesh.shape["fsdp"], mesh.shape["ctx"])
    return jax.shard_map(body, mesh=mesh, in_specs=placed, out_specs=P("fsdp", "ctx"), check_vma=False)
```

```python
import functools

import jax
import jax.numpy as jnp
from jax import lax
from jax.experimental import pallas as pl
from jax.experimental.pallas import tpu as pltpu
from jax.sharding import PartitionSpec as P

EPSILON = 1e-05
MESH = pl.DeviceIdType.MESH
LANES = 128
ROWS = 8


class Plan:
    def __init__(self, fsdp, ctx, rows, tokens, long_len):
        self.cores = 2
        self.ring = {64: 8, 16: 4, 8: 4}[fsdp]
        self.line = fsdp // (self.ring * self.cores)
        self.plane = self.line * self.cores
        self.fsdp, self.ctx = fsdp, ctx
        self.rows, self.tokens, self.long_len = rows, tokens, long_len
        self.half = self.ring // 2
        self.blocks = long_len // LANES
        self.token_tiles = tokens // LANES


def copy_to(src, dst, send, recv, device):
    return pltpu.make_async_remote_copy(
        src_ref=src, dst_ref=dst, send_sem=send, recv_sem=recv, device_id=device, device_id_type=MESH
    )


def kernel(
    plan, act, gain, w_in, w_short, filt, skip, w_out, out,
    gath, mixg, win, wout, xin, hin, hrow, tmat, acc, acc2, plane_sum, ring_sum,
    pbuf, rbuf, mbuf, mrecv, seq, gseq, fseq, skipb, tapb,
    lsem, plane_sem, ring_sem, zsem, ysem, lastsem, csem, zsem2, ysem2, lastsem2, csem2, asem, bsem,
):
    me = lax.axis_index("fsdp")
    ctx = lax.axis_index("ctx")
    ring, line, plane, half = plan.ring, plan.line, plan.plane, plan.half
    y = me // plane
    p = lax.rem(me, plane)
    z = p // plan.cores
    core = lax.rem(p, plan.cores)
    rows, tokens = plan.rows, plan.tokens

    def at(yy, zz, cc):
        return (yy * line + zz) * plan.cores + cc

    def turn(yy):
        return lax.rem(yy + 2 * ring, ring)

    loads = [
        pltpu.make_async_copy(act, xin, lsem.at[0]),
        pltpu.make_async_copy(filt.at[ctx], hin, lsem.at[1]),
        pltpu.make_async_copy(w_in, win, lsem.at[2]),
        pltpu.make_async_copy(w_out, wout, lsem.at[3]),
    ]
    for load in loads:
        load.start()

    barrier = pltpu.get_barrier_semaphore()

    def greet(device):
        pl.semaphore_signal(barrier, inc=1, device_id=device, device_id_type=MESH)

    @pl.loop(1, plane)
    def _(o):
        greet({"fsdp": y * plane + (p ^ o)})

    @pl.loop(1, ring)
    def _(o):
        greet({"fsdp": turn(y + o) * plane + p})

    if plan.ctx > 1:
        @pl.loop(1, plan.ctx)
        def _(o):
            greet({"ctx": ctx ^ o})

    def column(row):
        n = row.shape[1]
        same = lax.broadcasted_iota(jnp.int32, (n, n), 0) == lax.broadcasted_iota(jnp.int32, (n, n), 1)
        return jnp.sum(jnp.where(same, jnp.broadcast_to(row, (n, n)), 0.0), axis=1, keepdims=True)

    loads[0].wait()
    own = xin[...].astype(jnp.float32)
    gath[me] = (own * column(gain[...])).astype(jnp.bfloat16)
    squares = jnp.sum(own * own, axis=0, keepdims=True)
    plane_sum[0] = jnp.zeros((ROWS, LANES), jnp.float32)
    for k in range(plan.token_tiles):
        plane_sum[0, k : k + 1, :] = squares[:, k * LANES : (k + 1) * LANES]
    skipb[...] = jnp.broadcast_to(column(skip[...]), (rows, LANES))
    for k in range(9):
        tapb[k] = jnp.broadcast_to(column(w_short[k // 3, k % 3 : k % 3 + 1, :]), (rows, LANES))
    acc[...] = jnp.zeros_like(acc)
    acc2[...] = jnp.zeros_like(acc2)
    gseq[...] = jnp.zeros_like(gseq)
    seq[:, :, :LANES] = jnp.zeros((3, ROWS, LANES), jnp.float32)
    pl.semaphore_wait(barrier, (plane - 1) + (ring - 1) + (plan.ctx - 1))

    def plane_copy(o):
        return copy_to(
            plane_sum.at[0], plane_sum.at[o], plane_sem.at[0, o], plane_sem.at[1, o], {"fsdp": y * plane + (p ^ o)}
        )

    def ring_copy(o):
        return copy_to(
            ring_sum.at[0], ring_sum.at[o], ring_sem.at[0, o], ring_sem.at[1, o], {"fsdp": turn(y + o) * plane + p}
        )

    def gather(buf, zs, ys, bs, cs, multiply, fillers):
        first = rows - rows // 4
        last = ring - 1

        def place(r):
            if r < half:
                return turn(y - r)
            return turn(y + (r - half + 1)) if r < last else turn(y + half)

        def columns(s):
            return [s, half - 1 + s] if s < half else [last]

        def zcopy(o, zz_from):
            view = buf.at[at(y, zz_from, core), pl.ds(0, first)]
            return copy_to(view, view, zs.at[0, o], zs.at[1, o], {"fsdp": at(y, z ^ o, core)})

        def ycopy(r, o, yy, step, whole):
            block = at(yy, z ^ o, core)
            view = buf.at[block] if whole else buf.at[block, pl.ds(0, first)]
            return copy_to(view, view, ys.at[0, r, o], ys.at[1, r, o], {"fsdp": at(turn(y + step), z, core)})

        def bcopy(r, o, zz_from):
            view = buf.at[at(place(r), zz_from, core), pl.ds(first, rows - first)]
            return copy_to(view, view, bs.at[0, r, o], bs.at[1, r, o], {"fsdp": at(y, z ^ o, core)})

        def ccopy(r, o, cc):
            block = buf.at[at(place(r), z ^ o, cc)]
            return copy_to(block, block, cs.at[0, r, o], cs.at[1, r, o], {"fsdp": at(y, z, 1 - core)})

        def pass_on(d, s, o, whole):
            yy = turn(y - (s - 1)) if d == 0 else turn(y + (s - 1))
            copy = ycopy(columns(s)[d if s < half else 0], o, yy, 1 - 2 * d, whole)
            if s < half:
                copy.start()
            else:
                pl.when(core == d)(copy.start)

        def arrive(s, o):
            for d, r in enumerate(columns(s)):
                ycopy(r, o, place(r), 1, o == 0).wait_recv()
                if s < half:
                    pass_on(d, s + 1, o, o == 0)
                if o == 0:
                    spread_line(r)

        def spread_line(r):
            for k in range(1, line):
                bcopy(r, k, z).start()
            if r:
                ccopy(r, 0, core).start()

        def arrive_line(o):
            zcopy(o, z ^ o).wait_recv()
            for d in range(2):
                pass_on(d, 1, o, False)
            if o == 1:
                spread_line(0)

        def hand_over(s):
            for r in columns(s) if s else [0]:
                @pl.loop(1, line)
                def _(o):
                    bcopy(r, o, z ^ o).wait_recv()
                    ccopy(r, o, core).start()

        def finish(s):
            for r in columns(s) if s else [0]:
                @pl.loop(0, line)
                def _(o):
                    ccopy(r, o, 1 - core).wait_recv()

                multiply(place(r))

        def drain(s):
            for r in columns(s) if s else [0]:
                if s:
                    ycopy(r, 0, y, 1, True).wait_send()
                ccopy(r, 0, core).wait_send()

                @pl.loop(1, line)
                def _(o):
                    if s:
                        ycopy(r, o, y, 1, False).wait_send()
                    else:
                        zcopy(o, z).wait_send()
                    bcopy(r, o, z).wait_send()
                    ccopy(r, o, core).wait_send()

        for d in range(2):
            pass_on(d, 1, 0, True)
        for o in range(1, line):
            zcopy(o, z).start()
        ccopy(0, 0, core).start()

        hop = 4.8
        crossed = [0.0] + [2.0 + 2.2 * o for o in range(1, line)]
        events = list(fillers)
        for o in range(1, line):
            events.append((crossed[o], functools.partial(arrive_line, o)))
        for s in range(half + 1):
            for o in range(line if s else 0):
                events.append((crossed[o] + hop * s, functools.partial(arrive, s, o)))
            handed = max(crossed[-1] + hop * s, hop * (s + 1)) + 0.1
            events.append((handed, functools.partial(hand_over, s)))
            events.append((handed + 2.0, functools.partial(finish, s)))
            if s < half - 1:
                events.append((handed + 10.0, functools.partial(drain, s)))
        for _, event in sorted(events, key=lambda e: e[0]):
            event()

        def rest():
            drain(half - 1)
            drain(half)

        return rest

    width = plane * rows

    def multiply_in(yy):
        w = win[:, :, pl.ds(pl.multiple_of(yy * width, width), width)].reshape(3 * rows, width)
        x = gath[pl.ds(yy * plane, plane)].reshape(width, tokens)
        acc[...] += jnp.dot(w, x, preferred_element_type=jnp.float32)

    def multiply_out(yy):
        w = wout[:, pl.ds(pl.multiple_of(yy * width, width), width)]
        x = mixg[pl.ds(yy * plane, plane)].reshape(width, tokens)
        acc2[...] += jnp.dot(w, x, preferred_element_type=jnp.float32)

    def spread_filter():
        for load in loads[1:]:
            load.wait()
        h = hin[...].astype(jnp.float32)
        for d in range(plan.blocks):
            hrow[pl.ds(d, ROWS, stride=plan.blocks), :] = h[:, d * LANES : (d + 1) * LANES]

    later = lax.broadcasted_iota(jnp.int32, (LANES, LANES), 1) >= lax.broadcasted_iota(jnp.int32, (LANES, LANES), 0)

    def band(first, last):
        @pl.loop(first, last)
        def _(c):
            def body(d, before):
                r = c * plan.blocks + d
                line_ = jnp.broadcast_to(hrow[pl.ds(r, 1), :], (LANES, LANES))
                rolled = pltpu.roll(line_, 0, 1, stride=1, stride_axis=0)
                tmat[r] = jnp.where(later, rolled, before).astype(jnp.bfloat16)
                return rolled

            lax.fori_loop(0, plan.blocks, body, jnp.zeros((LANES, LANES), jnp.float32), unroll=min(8, plan.blocks))

    def start_plane():
        @pl.loop(1, plane)
        def _(o):
            plane_copy(o).start()

    def start_ring():
        @pl.loop(1, plane)
        def _(o):
            plane_copy(o).wait_recv()

        ring_sum[0] = jnp.sum(plane_sum[...], axis=0)

        @pl.loop(1, ring)
        def _(o):
            ring_copy(o).start()

    fillers = [(0.0, start_plane), (4.3, spread_filter), (8.3, start_ring)]
    fillers += [(7.0 + 1.9 * i, functools.partial(band, i, i + 1)) for i in range(ROWS)]
    drain1 = gather(gath, zsem, ysem, lastsem, csem, multiply_in, fillers)

    @pl.loop(1, ring)
    def _(o):
        ring_copy(o).wait_recv()

    features = plan.fsdp * rows
    factor = lax.rsqrt(jnp.sum(ring_sum[...], axis=0) / features + EPSILON)
    for k in range(plan.token_tiles):
        lanes = slice(k * LANES, (k + 1) * LANES)
        for s in range(3):
            scaled = acc[s * rows : (s + 1) * rows, lanes] * factor[k : k + 1, :]
            for j in range(plan.ctx):
                n = rows // plan.ctx
                pbuf[j, s, :, lanes] = scaled[j * n : (j + 1) * n].astype(jnp.bfloat16)

    def swap(src, dst, sem, meanwhile):
        def one(o):
            return copy_to(src.at[ctx ^ o], dst.at[ctx], sem.at[0, o], sem.at[1, o], {"ctx": ctx ^ o})

        def arrival(o):
            return copy_to(src.at[ctx ^ o], dst.at[ctx ^ o], sem.at[0, o], sem.at[1, o], {"ctx": ctx ^ o})

        if plan.ctx > 1:
            @pl.loop(1, plan.ctx)
            def _(o):
                one(o).start()

        dst[ctx] = src[ctx]
        meanwhile()
        if plan.ctx > 1:
            @pl.loop(1, plan.ctx)
            def _(o):
                arrival(o).wait_recv()

        def drain():
            if plan.ctx > 1:
                @pl.loop(1, plan.ctx)
                def _(o):
                    one(o).wait_send()

        return drain

    def drain_first():
        @pl.loop(1, plane)
        def _(o):
            plane_copy(o).wait_send()

        @pl.loop(1, ring)
        def _(o):
            ring_copy(o).wait_send()

        drain1()

    drain2 = swap(pbuf, rbuf, asem, drain_first)

    for j in range(plan.ctx):
        for s in range(3):
            seq[s, :, LANES + j * tokens : LANES + (j + 1) * tokens] = rbuf[j, s].astype(jnp.float32)

    def smooth(s):
        taps = [tapb[3 * s + k, pl.ds(ctx * ROWS, ROWS), :][:, 0:1] for k in range(3)]
        full = seq[s]
        total = taps[0] * full + taps[1] * pltpu.roll(full, 1, 1)
        total = total + taps[2] * pltpu.roll(full, 2, 1)
        return total[:, LANES:]

    gated = (smooth(1) * smooth(2)).astype(jnp.bfloat16).astype(jnp.float32)
    query = smooth(0)
    blocks = plan.blocks
    for b in range(blocks):
        gseq[pl.ds(blocks + b, ROWS, stride=2 * blocks), :] = gated[:, b * LANES : (b + 1) * LANES]

    @pl.loop(0, ROWS)
    def _(c):
        base = c * 2 * blocks + blocks
        lhs = jnp.concatenate(
            [gseq[pl.ds(base - d, blocks), :].astype(jnp.bfloat16) for d in range(blocks)], axis=1
        )
        rhs = tmat[pl.ds(c * blocks, blocks)].reshape(blocks * LANES, LANES)
        fseq[pl.ds(c * blocks, blocks), :] = jnp.dot(lhs, rhs, preferred_element_type=jnp.float32)

    direct = skipb[pl.ds(ctx * ROWS, ROWS), :]
    for b in range(blocks):
        lanes = slice(b * LANES, (b + 1) * LANES)
        value = query[:, lanes] * (fseq[pl.ds(b, ROWS, stride=blocks), :] + direct * gated[:, lanes])
        j, k = b // plan.token_tiles, b % plan.token_tiles
        mbuf[j, :, k * LANES : (k + 1) * LANES] = value.astype(jnp.bfloat16)

    drain3 = swap(mbuf, mrecv, bsem, drain2)
    mixg[me] = mrecv[...].astype(jnp.float32).reshape(rows, tokens).astype(jnp.bfloat16)

    drain4 = gather(mixg, zsem2, ysem2, lastsem2, csem2, multiply_out, [])
    out[...] = acc2[...].astype(jnp.bfloat16)
    drain3()
    drain4()


def shards(fsdp, ctx, activations, norm_gain, w_in, w_short, long_filter, skip_gain, w_out):
    rows, tokens = activations.shape
    long_len = long_filter.shape[1]
    plan = Plan(fsdp, ctx, rows, tokens, long_len)
    groups = rows // ROWS
    features = fsdp * rows
    bf16, f32 = jnp.bfloat16, jnp.float32
    dma = pltpu.SemaphoreType.DMA
    anywhere = pl.BlockSpec(memory_space=pl.ANY)
    here = pl.BlockSpec(memory_space=pltpu.VMEM)
    gather_sems = [
        dma((2, max(plan.line, 2))),
        dma((2, plan.ring, plan.line)),
        dma((2, plan.ring, max(plan.line, 2))),
        dma((2, plan.ring, plan.line)),
    ]
    scratch = [
        pltpu.VMEM((fsdp, rows, tokens), bf16),
        pltpu.VMEM((fsdp, rows, tokens), bf16),
        pltpu.VMEM((3, rows, features), bf16),
        pltpu.VMEM((rows, features), bf16),
        pltpu.VMEM((rows, tokens), bf16),
        pltpu.VMEM((ROWS, long_len), bf16),
        pltpu.VMEM((ROWS * plan.blocks, LANES), f32),
        pltpu.VMEM((ROWS * plan.blocks, LANES, LANES), bf16),
        pltpu.VMEM((3 * rows, tokens), f32),
        pltpu.VMEM((rows, tokens), f32),
        pltpu.VMEM((plan.plane, ROWS, LANES), f32),
        pltpu.VMEM((plan.ring, ROWS, LANES), f32),
        pltpu.VMEM((ctx, 3, ROWS, tokens), bf16),
        pltpu.VMEM((ctx, 3, ROWS, tokens), bf16),
        pltpu.VMEM((ctx, ROWS, tokens), bf16),
        pltpu.VMEM((ctx, ROWS, tokens), bf16),
        pltpu.VMEM((3, ROWS, LANES + long_len), f32),
        pltpu.VMEM((ROWS * 2 * plan.blocks, LANES), f32),
        pltpu.VMEM((ROWS * plan.blocks, LANES), f32),
        pltpu.VMEM((rows, LANES), f32),
        pltpu.VMEM((9, rows, LANES), f32),
        dma((4,)),
        dma((2, plan.plane)),
        dma((2, plan.ring)),
        *gather_sems,
        *gather_sems,
        dma((2, ctx)),
        dma((2, ctx)),
    ]
    return pl.pallas_call(
        functools.partial(kernel, plan),
        out_shape=jax.ShapeDtypeStruct((rows, tokens), bf16),
        in_specs=[anywhere, here, anywhere, here, anywhere, here, anywhere],
        out_specs=here,
        scratch_shapes=scratch,
        compiler_params=pltpu.CompilerParams(
            collective_id=0, has_side_effects=True, vmem_limit_bytes=56 * 1024 * 1024
        ),
        name="mixer",
    )(
        activations,
        norm_gain.reshape(1, rows),
        w_in,
        jnp.transpose(w_short, (0, 2, 1)),
        long_filter.reshape(groups, ROWS, long_len),
        skip_gain.reshape(1, rows),
        w_out,
    )


def solution(mesh):
    placed = (
        P("fsdp", "ctx"),
        P("fsdp"),
        P(None, "fsdp", None),
        P(None, "fsdp", None),
        P("fsdp", None),
        P("fsdp"),
        P("fsdp", None),
    )
    body = functools.partial(shards, mesh.shape["fsdp"], mesh.shape["ctx"])
    return jax.shard_map(body, mesh=mesh, in_specs=placed, out_specs=P("fsdp", "ctx"), check_vma=False)
```

```python
import functools

import jax
import jax.numpy as jnp
from jax import lax
from jax.experimental import pallas as pl
from jax.experimental.pallas import tpu as pltpu
from jax.sharding import PartitionSpec as P

EPSILON = 1e-05
MESH = pl.DeviceIdType.MESH
LANES = 128
ROWS = 8


class Plan:
    def __init__(self, fsdp, ctx, rows, tokens, long_len):
        self.cores = 2
        self.ring = {64: 8, 16: 4, 8: 4}[fsdp]
        self.line = fsdp // (self.ring * self.cores)
        self.plane = self.line * self.cores
        self.fsdp, self.ctx = fsdp, ctx
        self.rows, self.tokens, self.long_len = rows, tokens, long_len
        self.half = self.ring // 2
        self.blocks = long_len // LANES
        self.token_tiles = tokens // LANES


def copy_to(src, dst, send, recv, device):
    return pltpu.make_async_remote_copy(
        src_ref=src, dst_ref=dst, send_sem=send, recv_sem=recv, device_id=device, device_id_type=MESH
    )


def kernel(
    plan, act, gain, w_in, w_short, filt, skip, w_out, out,
    gath, mixg, win, wout, xin, hin, hrow, tmat, acc, acc2, plane_sum, ring_sum,
    pbuf, rbuf, qbuf, qrecv, mbuf, mrecv, seq, gseq, fseq, skipb, tapb,
    lsem, plane_sem, ring_sem, zsem, ysem, lastsem, csem, zsem2, ysem2, lastsem2, csem2, asem, qsem, bsem,
):
    me = lax.axis_index("fsdp")
    ctx = lax.axis_index("ctx")
    ring, line, plane, half = plan.ring, plan.line, plan.plane, plan.half
    y = me // plane
    p = lax.rem(me, plane)
    z = p // plan.cores
    core = lax.rem(p, plan.cores)
    rows, tokens = plan.rows, plan.tokens

    def at(yy, zz, cc):
        return (yy * line + zz) * plan.cores + cc

    def turn(yy):
        return lax.rem(yy + 2 * ring, ring)

    loads = [
        pltpu.make_async_copy(act, xin, lsem.at[0]),
        pltpu.make_async_copy(filt.at[ctx], hin, lsem.at[1]),
        pltpu.make_async_copy(w_in, win, lsem.at[2]),
        pltpu.make_async_copy(w_out, wout, lsem.at[3]),
    ]
    for load in loads:
        load.start()

    barrier = pltpu.get_barrier_semaphore()

    def greet(device):
        pl.semaphore_signal(barrier, inc=1, device_id=device, device_id_type=MESH)

    @pl.loop(1, plane)
    def _(o):
        greet({"fsdp": y * plane + (p ^ o)})

    @pl.loop(1, ring)
    def _(o):
        greet({"fsdp": turn(y + o) * plane + p})

    if plan.ctx > 1:
        @pl.loop(1, plan.ctx)
        def _(o):
            greet({"ctx": ctx ^ o})

    def column(row):
        n = row.shape[1]
        same = lax.broadcasted_iota(jnp.int32, (n, n), 0) == lax.broadcasted_iota(jnp.int32, (n, n), 1)
        return jnp.sum(jnp.where(same, jnp.broadcast_to(row, (n, n)), 0.0), axis=1, keepdims=True)

    loads[0].wait()
    own = xin[...].astype(jnp.float32)
    gath[me] = (own * column(gain[...])).astype(jnp.bfloat16)
    squares = jnp.sum(own * own, axis=0, keepdims=True)
    plane_sum[0] = jnp.zeros((ROWS, LANES), jnp.float32)
    for k in range(plan.token_tiles):
        plane_sum[0, k : k + 1, :] = squares[:, k * LANES : (k + 1) * LANES]
    skipb[...] = jnp.broadcast_to(column(skip[...]), (rows, LANES))
    for k in range(9):
        tapb[k] = jnp.broadcast_to(column(w_short[k // 3, k % 3 : k % 3 + 1, :]), (rows, LANES))
    acc[...] = jnp.zeros_like(acc)
    acc2[...] = jnp.zeros_like(acc2)
    gseq[...] = jnp.zeros_like(gseq)
    seq[:, :, :LANES] = jnp.zeros((3, ROWS, LANES), jnp.float32)
    pl.semaphore_wait(barrier, (plane - 1) + (ring - 1) + (plan.ctx - 1))

    def plane_copy(o):
        return copy_to(
            plane_sum.at[0], plane_sum.at[o], plane_sem.at[0, o], plane_sem.at[1, o], {"fsdp": y * plane + (p ^ o)}
        )

    def ring_copy(o):
        return copy_to(
            ring_sum.at[0], ring_sum.at[o], ring_sem.at[0, o], ring_sem.at[1, o], {"fsdp": turn(y + o) * plane + p}
        )

    def gather(buf, zs, ys, bs, cs, multiply, fillers):
        first = rows - rows // 4
        last = ring - 1

        def place(r):
            if r < half:
                return turn(y - r)
            return turn(y + (r - half + 1)) if r < last else turn(y + half)

        def columns(s):
            return [s, half - 1 + s] if s < half else [last]

        def zcopy(o, zz_from):
            view = buf.at[at(y, zz_from, core), pl.ds(0, first)]
            return copy_to(view, view, zs.at[0, o], zs.at[1, o], {"fsdp": at(y, z ^ o, core)})

        def ycopy(r, o, yy, step, whole):
            block = at(yy, z ^ o, core)
            view = buf.at[block] if whole else buf.at[block, pl.ds(0, first)]
            return copy_to(view, view, ys.at[0, r, o], ys.at[1, r, o], {"fsdp": at(turn(y + step), z, core)})

        def bcopy(r, o, zz_from):
            view = buf.at[at(place(r), zz_from, core), pl.ds(first, rows - first)]
            return copy_to(view, view, bs.at[0, r, o], bs.at[1, r, o], {"fsdp": at(y, z ^ o, core)})

        def ccopy(r, o, cc):
            block = buf.at[at(place(r), z ^ o, cc)]
            return copy_to(block, block, cs.at[0, r, o], cs.at[1, r, o], {"fsdp": at(y, z, 1 - core)})

        def pass_on(d, s, o, whole):
            yy = turn(y - (s - 1)) if d == 0 else turn(y + (s - 1))
            copy = ycopy(columns(s)[d if s < half else 0], o, yy, 1 - 2 * d, whole)
            if s < half:
                copy.start()
            else:
                pl.when(core == d)(copy.start)

        def arrive(s, o):
            for d, r in enumerate(columns(s)):
                ycopy(r, o, place(r), 1, o == 0).wait_recv()
                if s < half:
                    pass_on(d, s + 1, o, o == 0)
                if o == 0:
                    spread_line(r)

        def spread_line(r):
            for k in range(1, line):
                bcopy(r, k, z).start()
            if r:
                ccopy(r, 0, core).start()

        def arrive_line(o):
            zcopy(o, z ^ o).wait_recv()
            for d in range(2):
                pass_on(d, 1, o, False)
            if o == 1:
                spread_line(0)

        def hand_over(s, o):
            for r in columns(s) if s else [0]:
                bcopy(r, o, z ^ o).wait_recv()
                ccopy(r, o, core).start()

        def finish(s):
            for r in columns(s) if s else [0]:
                @pl.loop(0, line)
                def _(o):
                    ccopy(r, o, 1 - core).wait_recv()

                multiply(place(r))

        def drain(s):
            for r in columns(s) if s else [0]:
                if s:
                    ycopy(r, 0, y, 1, True).wait_send()
                ccopy(r, 0, core).wait_send()

                @pl.loop(1, line)
                def _(o):
                    if s:
                        ycopy(r, o, y, 1, False).wait_send()
                    else:
                        zcopy(o, z).wait_send()
                    bcopy(r, o, z).wait_send()
                    ccopy(r, o, core).wait_send()

        for d in range(2):
            pass_on(d, 1, 0, True)
        for o in range(1, line):
            zcopy(o, z).start()
        ccopy(0, 0, core).start()

        hop = 5.6
        crossed = [0.0] + [2.0 + 2.2 * o for o in range(1, line)]
        events = list(fillers)
        for o in range(1, line):
            events.append((crossed[o], functools.partial(arrive_line, o)))
        for s in range(half + 1):
            for o in range(line if s else 0):
                events.append((crossed[o] + hop * s, functools.partial(arrive, s, o)))
            for o in range(1, line):
                handed = max(crossed[o] + hop * s, hop * (s + 1)) + 0.1
                events.append((handed, functools.partial(hand_over, s, o)))
            handed = max(crossed[-1] + hop * s, hop * (s + 1)) + 0.1
            events.append((handed + 2.0, functools.partial(finish, s)))
            if s < half - 1:
                events.append((handed + 10.0, functools.partial(drain, s)))
        for _, event in sorted(events, key=lambda e: e[0]):
            event()

        def rest():
            drain(half - 1)
            drain(half)

        return rest

    width = plane * rows

    def multiply_in(yy):
        w = win[:, :, pl.ds(pl.multiple_of(yy * width, width), width)].reshape(3 * rows, width)
        x = gath[pl.ds(yy * plane, plane)].reshape(width, tokens)
        acc[...] += jnp.dot(w, x, preferred_element_type=jnp.float32)

    def multiply_out(yy):
        w = wout[:, pl.ds(pl.multiple_of(yy * width, width), width)]
        x = mixg[pl.ds(yy * plane, plane)].reshape(width, tokens)
        acc2[...] += jnp.dot(w, x, preferred_element_type=jnp.float32)

    def spread_filter():
        for load in loads[1:]:
            load.wait()
        h = hin[...].astype(jnp.float32)
        for d in range(plan.blocks):
            hrow[pl.ds(d, ROWS, stride=plan.blocks), :] = h[:, d * LANES : (d + 1) * LANES]

    later = lax.broadcasted_iota(jnp.int32, (LANES, LANES), 1) >= lax.broadcasted_iota(jnp.int32, (LANES, LANES), 0)

    def band(first, last):
        @pl.loop(first, last)
        def _(c):
            def body(d, before):
                r = c * plan.blocks + d
                line_ = jnp.broadcast_to(hrow[pl.ds(r, 1), :], (LANES, LANES))
                rolled = pltpu.roll(line_, 0, 1, stride=1, stride_axis=0)
                tmat[r] = jnp.where(later, rolled, before).astype(jnp.bfloat16)
                return rolled

            lax.fori_loop(0, plan.blocks, body, jnp.zeros((LANES, LANES), jnp.float32), unroll=min(8, plan.blocks))

    def start_plane():
        @pl.loop(1, plane)
        def _(o):
            plane_copy(o).start()

    def start_ring():
        @pl.loop(1, plane)
        def _(o):
            plane_copy(o).wait_recv()

        ring_sum[0] = jnp.sum(plane_sum[...], axis=0)

        @pl.loop(1, ring)
        def _(o):
            ring_copy(o).start()

    fillers = [(0.0, start_plane), (4.3, spread_filter), (8.3, start_ring)]
    fillers += [(7.0 + 1.9 * i, functools.partial(band, i, i + 1)) for i in range(ROWS)]
    drain1 = gather(gath, zsem, ysem, lastsem, csem, multiply_in, fillers)

    @pl.loop(1, ring)
    def _(o):
        ring_copy(o).wait_recv()

    features = plan.fsdp * rows
    factor = lax.rsqrt(jnp.sum(ring_sum[...], axis=0) / features + EPSILON)

    def project(s, store):
        for k in range(plan.token_tiles):
            lanes = slice(k * LANES, (k + 1) * LANES)
            scaled = acc[s * rows : (s + 1) * rows, lanes] * factor[k : k + 1, :]
            for j in range(plan.ctx):
                store(j, lanes, scaled[j * ROWS : (j + 1) * ROWS].astype(jnp.bfloat16))

    def keep_key(j, lanes, value):
        pbuf[j, 0, :, lanes] = value

    def keep_value(j, lanes, value):
        pbuf[j, 1, :, lanes] = value

    def keep_query(j, lanes, value):
        qbuf[j, :, lanes] = value

    def swap(src, dst, sem):
        order = [o for o in range(1, plan.ctx) if o % 2] + [o for o in range(2, plan.ctx, 2)]

        def copy(o, slot):
            return copy_to(src.at[ctx ^ o], dst.at[slot], sem.at[0, o], sem.at[1, o], {"ctx": ctx ^ o})

        for o in order:
            copy(o, ctx).start()
        dst[ctx] = src[ctx]

        def arrive():
            for o in order:
                copy(o, ctx ^ o).wait_recv()

        def drain():
            for o in order:
                copy(o, ctx).wait_send()

        return arrive, drain

    project(1, keep_key)
    project(2, keep_value)
    arrive_gate, drain_gate = swap(pbuf, rbuf, asem)
    project(0, keep_query)
    arrive_query, drain_query = swap(qbuf, qrecv, qsem)

    @pl.loop(1, plane)
    def _(o):
        plane_copy(o).wait_send()

    @pl.loop(1, ring)
    def _(o):
        ring_copy(o).wait_send()

    drain1()
    arrive_gate()

    for j in range(plan.ctx):
        for s in range(2):
            seq[s + 1, :, LANES + j * tokens : LANES + (j + 1) * tokens] = rbuf[j, s].astype(jnp.float32)

    def smooth(s):
        taps = [tapb[3 * s + k, pl.ds(ctx * ROWS, ROWS), :][:, 0:1] for k in range(3)]
        full = seq[s]
        total = taps[0] * full + taps[1] * pltpu.roll(full, 1, 1)
        total = total + taps[2] * pltpu.roll(full, 2, 1)
        return total[:, LANES:]

    gated = (smooth(1) * smooth(2)).astype(jnp.bfloat16).astype(jnp.float32)
    blocks = plan.blocks
    for b in range(blocks):
        gseq[pl.ds(blocks + b, ROWS, stride=2 * blocks), :] = gated[:, b * LANES : (b + 1) * LANES]

    @pl.loop(0, ROWS)
    def _(c):
        base = c * 2 * blocks + blocks
        lhs = jnp.concatenate(
            [gseq[pl.ds(base - d, blocks), :].astype(jnp.bfloat16) for d in range(blocks)], axis=1
        )
        rhs = tmat[pl.ds(c * blocks, blocks)].reshape(blocks * LANES, LANES)
        fseq[pl.ds(c * blocks, blocks), :] = jnp.dot(lhs, rhs, preferred_element_type=jnp.float32)

    arrive_query()
    for j in range(plan.ctx):
        seq[0, :, LANES + j * tokens : LANES + (j + 1) * tokens] = qrecv[j].astype(jnp.float32)
    query = smooth(0)
    direct = skipb[pl.ds(ctx * ROWS, ROWS), :]
    for b in range(blocks):
        lanes = slice(b * LANES, (b + 1) * LANES)
        value = query[:, lanes] * (fseq[pl.ds(b, ROWS, stride=blocks), :] + direct * gated[:, lanes])
        j, k = b // plan.token_tiles, b % plan.token_tiles
        mbuf[j, :, k * LANES : (k + 1) * LANES] = value.astype(jnp.bfloat16)

    arrive_mixed, drain_mixed = swap(mbuf, mrecv, bsem)
    drain_gate()
    drain_query()
    arrive_mixed()
    mixg[me] = mrecv[...].astype(jnp.float32).reshape(rows, tokens).astype(jnp.bfloat16)

    drain4 = gather(mixg, zsem2, ysem2, lastsem2, csem2, multiply_out, [])
    out[...] = acc2[...].astype(jnp.bfloat16)
    drain_mixed()
    drain4()


def shards(fsdp, ctx, activations, norm_gain, w_in, w_short, long_filter, skip_gain, w_out):
    rows, tokens = activations.shape
    long_len = long_filter.shape[1]
    plan = Plan(fsdp, ctx, rows, tokens, long_len)
    groups = rows // ROWS
    features = fsdp * rows
    bf16, f32 = jnp.bfloat16, jnp.float32
    dma = pltpu.SemaphoreType.DMA
    anywhere = pl.BlockSpec(memory_space=pl.ANY)
    here = pl.BlockSpec(memory_space=pltpu.VMEM)
    gather_sems = [
        dma((2, max(plan.line, 2))),
        dma((2, plan.ring, plan.line)),
        dma((2, plan.ring, max(plan.line, 2))),
        dma((2, plan.ring, plan.line)),
    ]
    scratch = [
        pltpu.VMEM((fsdp, rows, tokens), bf16),
        pltpu.VMEM((fsdp, rows, tokens), bf16),
        pltpu.VMEM((3, rows, features), bf16),
        pltpu.VMEM((rows, features), bf16),
        pltpu.VMEM((rows, tokens), bf16),
        pltpu.VMEM((ROWS, long_len), bf16),
        pltpu.VMEM((ROWS * plan.blocks, LANES), f32),
        pltpu.VMEM((ROWS * plan.blocks, LANES, LANES), bf16),
        pltpu.VMEM((3 * rows, tokens), f32),
        pltpu.VMEM((rows, tokens), f32),
        pltpu.VMEM((plan.plane, ROWS, LANES), f32),
        pltpu.VMEM((plan.ring, ROWS, LANES), f32),
        pltpu.VMEM((ctx, 2, ROWS, tokens), bf16),
        pltpu.VMEM((ctx, 2, ROWS, tokens), bf16),
        pltpu.VMEM((ctx, ROWS, tokens), bf16),
        pltpu.VMEM((ctx, ROWS, tokens), bf16),
        pltpu.VMEM((ctx, ROWS, tokens), bf16),
        pltpu.VMEM((ctx, ROWS, tokens), bf16),
        pltpu.VMEM((3, ROWS, LANES + long_len), f32),
        pltpu.VMEM((ROWS * 2 * plan.blocks, LANES), f32),
        pltpu.VMEM((ROWS * plan.blocks, LANES), f32),
        pltpu.VMEM((rows, LANES), f32),
        pltpu.VMEM((9, rows, LANES), f32),
        dma((4,)),
        dma((2, plan.plane)),
        dma((2, plan.ring)),
        *gather_sems,
        *gather_sems,
        dma((2, ctx)),
        dma((2, ctx)),
        dma((2, ctx)),
    ]
    return pl.pallas_call(
        functools.partial(kernel, plan),
        out_shape=jax.ShapeDtypeStruct((rows, tokens), bf16),
        in_specs=[anywhere, here, anywhere, here, anywhere, here, anywhere],
        out_specs=here,
        scratch_shapes=scratch,
        compiler_params=pltpu.CompilerParams(
            collective_id=0, has_side_effects=True, vmem_limit_bytes=56 * 1024 * 1024
        ),
        name="mixer",
    )(
        activations,
        norm_gain.reshape(1, rows),
        w_in,
        jnp.transpose(w_short, (0, 2, 1)),
        long_filter.reshape(groups, ROWS, long_len),
        skip_gain.reshape(1, rows),
        w_out,
    )


def solution(mesh):
    placed = (
        P("fsdp", "ctx"),
        P("fsdp"),
        P(None, "fsdp", None),
        P(None, "fsdp", None),
        P("fsdp", None),
        P("fsdp"),
        P("fsdp", None),
    )
    body = functools.partial(shards, mesh.shape["fsdp"], mesh.shape["ctx"])
    return jax.shard_map(body, mesh=mesh, in_specs=placed, out_specs=P("fsdp", "ctx"), check_vma=False)
```

```python
import functools

import jax
import jax.numpy as jnp
from jax import lax
from jax.experimental import pallas as pl
from jax.experimental.pallas import tpu as pltpu
from jax.sharding import PartitionSpec as P

EPSILON = 1e-05
MESH = pl.DeviceIdType.MESH
LANES = 128
ROWS = 8


class Plan:
    def __init__(self, fsdp, ctx, rows, tokens, long_len):
        self.cores = 2
        self.ring = {64: 8, 16: 4, 8: 4}[fsdp]
        self.line = fsdp // (self.ring * self.cores)
        self.plane = self.line * self.cores
        self.fsdp, self.ctx = fsdp, ctx
        self.rows, self.tokens, self.long_len = rows, tokens, long_len
        self.half = self.ring // 2
        self.blocks = long_len // LANES
        self.token_tiles = tokens // LANES


def copy_to(src, dst, send, recv, device):
    return pltpu.make_async_remote_copy(
        src_ref=src, dst_ref=dst, send_sem=send, recv_sem=recv, device_id=device, device_id_type=MESH
    )


def kernel(
    plan, act, gain, w_in, w_short, filt, skip, w_out, out,
    gath, mixg, win, wout, xin, hin, hrow, tmat, acc, acc2, plane_sum, ring_sum, scale,
    pbuf, rbuf, qbuf, qrecv, mbuf, mrecv, seq, gseq, fseq, skipb, tapb,
    lsem, plane_sem, ring_sem, zsem, ysem, lastsem, csem, zsem2, ysem2, lastsem2, csem2, asem, qsem, bsem,
):
    me = lax.axis_index("fsdp")
    ctx = lax.axis_index("ctx")
    ring, line, plane, half = plan.ring, plan.line, plan.plane, plan.half
    y = me // plane
    p = lax.rem(me, plane)
    z = p // plan.cores
    core = lax.rem(p, plan.cores)
    rows, tokens = plan.rows, plan.tokens

    def at(yy, zz, cc):
        return (yy * line + zz) * plan.cores + cc

    def turn(yy):
        return lax.rem(yy + 2 * ring, ring)

    loads = [
        pltpu.make_async_copy(act, xin, lsem.at[0]),
        pltpu.make_async_copy(filt.at[ctx], hin, lsem.at[1]),
        pltpu.make_async_copy(w_in, win, lsem.at[2]),
        pltpu.make_async_copy(w_out, wout, lsem.at[3]),
    ]
    loads[0].start()
    barrier = pltpu.get_barrier_semaphore()

    def greet(device):
        pl.semaphore_signal(barrier, inc=1, device_id=device, device_id_type=MESH)

    for o in [o for o in range(1, plan.ctx) if o % 2] + [o for o in range(2, plan.ctx, 2)]:
        greet({"ctx": ctx ^ o})

    @pl.loop(1, ring)
    def _(o):
        greet({"fsdp": turn(y + o) * plane + p})

    @pl.loop(1, plane)
    def _(o):
        greet({"fsdp": y * plane + (p ^ o)})

    for load in loads[1:]:
        load.start()

    def column(row):
        n = row.shape[1]
        same = lax.broadcasted_iota(jnp.int32, (n, n), 0) == lax.broadcasted_iota(jnp.int32, (n, n), 1)
        return jnp.sum(jnp.where(same, jnp.broadcast_to(row, (n, n)), 0.0), axis=1, keepdims=True)

    loads[0].wait()
    own = xin[...].astype(jnp.float32)
    gath[me] = (own * column(gain[...])).astype(jnp.bfloat16)
    squares = jnp.sum(own * own, axis=0, keepdims=True)
    plane_sum[0] = jnp.zeros((ROWS, LANES), jnp.float32)
    for k in range(plan.token_tiles):
        plane_sum[0, k : k + 1, :] = squares[:, k * LANES : (k + 1) * LANES]
    skipb[...] = jnp.broadcast_to(column(skip[...]), (rows, LANES))
    for k in range(9):
        tapb[k] = jnp.broadcast_to(column(w_short[k // 3, k % 3 : k % 3 + 1, :]), (rows, LANES))
    acc[...] = jnp.zeros_like(acc)
    acc2[...] = jnp.zeros_like(acc2)
    gseq[...] = jnp.zeros_like(gseq)
    seq[:, :, :LANES] = jnp.zeros((3, ROWS, LANES), jnp.float32)
    pl.semaphore_wait(barrier, (plane - 1) + (ring - 1) + (plan.ctx - 1))

    def plane_copy(o):
        return copy_to(
            plane_sum.at[0], plane_sum.at[o], plane_sem.at[0, o], plane_sem.at[1, o], {"fsdp": y * plane + (p ^ o)}
        )

    def ring_copy(o):
        return copy_to(
            ring_sum.at[0], ring_sum.at[o], ring_sem.at[0, o], ring_sem.at[1, o], {"fsdp": turn(y + o) * plane + p}
        )

    def gather(buf, zs, ys, bs, cs, multiply, fillers):
        first = rows - rows // 4
        last = ring - 1

        def place(r):
            if r < half:
                return turn(y - r)
            return turn(y + (r - half + 1)) if r < last else turn(y + half)

        def columns(s):
            return [s, half - 1 + s] if s < half else [last]

        def zcopy(o, zz_from):
            view = buf.at[at(y, zz_from, core), pl.ds(0, first)]
            return copy_to(view, view, zs.at[0, o], zs.at[1, o], {"fsdp": at(y, z ^ o, core)})

        def ycopy(r, o, yy, step, whole):
            block = at(yy, z ^ o, core)
            view = buf.at[block] if whole else buf.at[block, pl.ds(0, first)]
            return copy_to(view, view, ys.at[0, r, o], ys.at[1, r, o], {"fsdp": at(turn(y + step), z, core)})

        def bcopy(r, o, zz_from):
            view = buf.at[at(place(r), zz_from, core), pl.ds(first, rows - first)]
            return copy_to(view, view, bs.at[0, r, o], bs.at[1, r, o], {"fsdp": at(y, z ^ o, core)})

        def ccopy(r, o, cc):
            block = buf.at[at(place(r), z ^ o, cc)]
            return copy_to(block, block, cs.at[0, r, o], cs.at[1, r, o], {"fsdp": at(y, z, 1 - core)})

        def pass_on(d, s, o, whole):
            yy = turn(y - (s - 1)) if d == 0 else turn(y + (s - 1))
            copy = ycopy(columns(s)[d if s < half else 0], o, yy, 1 - 2 * d, whole)
            if s < half:
                copy.start()
            else:
                pl.when(core == d)(copy.start)

        def arrive(s, o):
            for d, r in enumerate(columns(s)):
                ycopy(r, o, place(r), 1, o == 0).wait_recv()
                if s < half:
                    pass_on(d, s + 1, o, o == 0)
                if o == 0:
                    spread_line(r)

        def spread_line(r):
            for k in range(1, line):
                bcopy(r, k, z).start()
            if r:
                ccopy(r, 0, core).start()

        def arrive_line(o):
            zcopy(o, z ^ o).wait_recv()
            for d in range(2):
                pass_on(d, 1, o, False)
            if o == 1:
                spread_line(0)

        def hand_over(s, o):
            for r in columns(s) if s else [0]:
                bcopy(r, o, z ^ o).wait_recv()
                ccopy(r, o, core).start()

        def finish(s):
            for r in columns(s) if s else [0]:
                @pl.loop(0, line)
                def _(o):
                    ccopy(r, o, 1 - core).wait_recv()

                multiply(place(r))

        def drain(s):
            for r in columns(s) if s else [0]:
                if s:
                    ycopy(r, 0, y, 1, True).wait_send()
                ccopy(r, 0, core).wait_send()

                @pl.loop(1, line)
                def _(o):
                    if s:
                        ycopy(r, o, y, 1, False).wait_send()
                    else:
                        zcopy(o, z).wait_send()
                    bcopy(r, o, z).wait_send()
                    ccopy(r, o, core).wait_send()

        for d in range(2):
            pass_on(d, 1, 0, True)
        for o in range(1, line):
            zcopy(o, z).start()
        ccopy(0, 0, core).start()

        hop = 5.6
        crossed = [0.0] + [2.0 + 2.2 * o for o in range(1, line)]
        events = list(fillers)
        for o in range(1, line):
            events.append((crossed[o], functools.partial(arrive_line, o)))
        for s in range(half + 1):
            for o in range(line if s else 0):
                events.append((crossed[o] + hop * s, functools.partial(arrive, s, o)))
            for o in range(1, line):
                handed = max(crossed[o] + hop * s, hop * (s + 1)) + 0.1
                events.append((handed, functools.partial(hand_over, s, o)))
            handed = max(crossed[-1] + hop * s, hop * (s + 1)) + 0.1
            events.append((handed + 2.0, functools.partial(finish, s)))
            if s == half:
                events.append((handed + 1.0, functools.partial(drain, s - 1)))
            elif s < half - 1:
                events.append((handed + 10.0, functools.partial(drain, s)))
        for _, event in sorted(events, key=lambda e: e[0]):
            event()

        return functools.partial(drain, half)

    width = plane * rows

    def multiply_in(yy):
        w = win[:, :, pl.ds(pl.multiple_of(yy * width, width), width)].reshape(3 * rows, width)
        x = gath[pl.ds(yy * plane, plane)].reshape(width, tokens)
        acc[...] += jnp.dot(w, x, preferred_element_type=jnp.float32)

    def multiply_out(yy):
        w = wout[:, pl.ds(pl.multiple_of(yy * width, width), width)]
        x = mixg[pl.ds(yy * plane, plane)].reshape(width, tokens)
        acc2[...] += jnp.dot(w, x, preferred_element_type=jnp.float32)

    def spread_filter():
        for load in loads[1:]:
            load.wait()
        h = hin[...].astype(jnp.float32)
        for d in range(plan.blocks):
            hrow[pl.ds(d, ROWS, stride=plan.blocks), :] = h[:, d * LANES : (d + 1) * LANES]

    later = lax.broadcasted_iota(jnp.int32, (LANES, LANES), 1) >= lax.broadcasted_iota(jnp.int32, (LANES, LANES), 0)

    def band(first, last):
        @pl.loop(first, last)
        def _(c):
            def body(d, before):
                r = c * plan.blocks + d
                line_ = jnp.broadcast_to(hrow[pl.ds(r, 1), :], (LANES, LANES))
                rolled = pltpu.roll(line_, 0, 1, stride=1, stride_axis=0)
                tmat[r] = jnp.where(later, rolled, before).astype(jnp.bfloat16)
                return rolled

            lax.fori_loop(0, plan.blocks, body, jnp.zeros((LANES, LANES), jnp.float32), unroll=min(8, plan.blocks))

    def start_plane():
        @pl.loop(1, plane)
        def _(o):
            plane_copy(o).start()

    def start_ring():
        @pl.loop(1, plane)
        def _(o):
            plane_copy(o).wait_recv()

        ring_sum[0] = jnp.sum(plane_sum[...], axis=0)

        @pl.loop(1, ring)
        def _(o):
            ring_copy(o).start()

    def end_sum():
        @pl.loop(1, ring)
        def _(o):
            ring_copy(o).wait_recv()

        scale[...] = lax.rsqrt(jnp.sum(ring_sum[...], axis=0) / (plan.fsdp * rows) + EPSILON)

    fillers = [(21.0, end_sum), (0.0, start_plane), (4.3, spread_filter), (8.3, start_ring)]
    fillers += [(7.0 + 1.9 * i, functools.partial(band, i, i + 1)) for i in range(ROWS)]
    drain1 = gather(gath, zsem, ysem, lastsem, csem, multiply_in, fillers)

    factor = scale[...]

    def project(s, store):
        for k in range(plan.token_tiles):
            lanes = slice(k * LANES, (k + 1) * LANES)
            scaled = acc[s * rows : (s + 1) * rows, lanes] * factor[k : k + 1, :]
            for j in range(plan.ctx):
                store(j, lanes, scaled[j * ROWS : (j + 1) * ROWS].astype(jnp.bfloat16))

    def keep_key(j, lanes, value):
        pbuf[j, 0, :, lanes] = value

    def keep_value(j, lanes, value):
        pbuf[j, 1, :, lanes] = value

    def keep_query(j, lanes, value):
        qbuf[j, :, lanes] = value

    def swap(src, dst, sem):
        order = [o for o in range(1, plan.ctx) if o % 2] + [o for o in range(2, plan.ctx, 2)]

        def copy(o, slot):
            return copy_to(src.at[ctx ^ o], dst.at[slot], sem.at[0, o], sem.at[1, o], {"ctx": ctx ^ o})

        for o in order:
            copy(o, ctx).start()
        dst[ctx] = src[ctx]

        def arrive():
            for o in order:
                copy(o, ctx ^ o).wait_recv()

        def drain():
            for o in order:
                copy(o, ctx).wait_send()

        return arrive, drain

    project(1, keep_key)
    project(2, keep_value)
    arrive_gate, drain_gate = swap(pbuf, rbuf, asem)
    project(0, keep_query)
    arrive_query, drain_query = swap(qbuf, qrecv, qsem)

    @pl.loop(1, plane)
    def _(o):
        plane_copy(o).wait_send()

    @pl.loop(1, ring)
    def _(o):
        ring_copy(o).wait_send()

    drain1()
    arrive_gate()

    for j in range(plan.ctx):
        for s in range(2):
            seq[s + 1, :, LANES + j * tokens : LANES + (j + 1) * tokens] = rbuf[j, s].astype(jnp.float32)

    def smooth(s):
        taps = [tapb[3 * s + k, pl.ds(ctx * ROWS, ROWS), :][:, 0:1] for k in range(3)]
        full = seq[s]
        total = taps[0] * full + taps[1] * pltpu.roll(full, 1, 1)
        total = total + taps[2] * pltpu.roll(full, 2, 1)
        return total[:, LANES:]

    gated = (smooth(1) * smooth(2)).astype(jnp.bfloat16).astype(jnp.float32)
    blocks = plan.blocks
    for b in range(blocks):
        gseq[pl.ds(blocks + b, ROWS, stride=2 * blocks), :] = gated[:, b * LANES : (b + 1) * LANES]

    @pl.loop(0, ROWS, unroll=2)
    def _(c):
        base = c * 2 * blocks + blocks
        lhs = jnp.concatenate(
            [gseq[pl.ds(base - d, blocks), :].astype(jnp.bfloat16) for d in range(blocks)], axis=1
        )
        rhs = tmat[pl.ds(c * blocks, blocks)].reshape(blocks * LANES, LANES)
        fseq[pl.ds(c * blocks, blocks), :] = jnp.dot(lhs, rhs, preferred_element_type=jnp.float32)

    arrive_query()
    for j in range(plan.ctx):
        seq[0, :, LANES + j * tokens : LANES + (j + 1) * tokens] = qrecv[j].astype(jnp.float32)
    query = smooth(0)
    direct = skipb[pl.ds(ctx * ROWS, ROWS), :]
    for b in range(blocks):
        lanes = slice(b * LANES, (b + 1) * LANES)
        value = query[:, lanes] * (fseq[pl.ds(b, ROWS, stride=blocks), :] + direct * gated[:, lanes])
        j, k = b // plan.token_tiles, b % plan.token_tiles
        mbuf[j, :, k * LANES : (k + 1) * LANES] = value.astype(jnp.bfloat16)

    arrive_mixed, drain_mixed = swap(mbuf, mrecv, bsem)
    drain_gate()
    drain_query()
    arrive_mixed()
    mixg[me] = mrecv[...].astype(jnp.float32).reshape(rows, tokens).astype(jnp.bfloat16)

    drain4 = gather(mixg, zsem2, ysem2, lastsem2, csem2, multiply_out, [])
    out[...] = acc2[...].astype(jnp.bfloat16)
    drain_mixed()
    drain4()


def shards(fsdp, ctx, activations, norm_gain, w_in, w_short, long_filter, skip_gain, w_out):
    rows, tokens = activations.shape
    long_len = long_filter.shape[1]
    plan = Plan(fsdp, ctx, rows, tokens, long_len)
    groups = rows // ROWS
    features = fsdp * rows
    bf16, f32 = jnp.bfloat16, jnp.float32
    dma = pltpu.SemaphoreType.DMA
    anywhere = pl.BlockSpec(memory_space=pl.ANY)
    here = pl.BlockSpec(memory_space=pltpu.VMEM)
    gather_sems = [
        dma((2, max(plan.line, 2))),
        dma((2, plan.ring, plan.line)),
        dma((2, plan.ring, max(plan.line, 2))),
        dma((2, plan.ring, plan.line)),
    ]
    scratch = [
        pltpu.VMEM((fsdp, rows, tokens), bf16),
        pltpu.VMEM((fsdp, rows, tokens), bf16),
        pltpu.VMEM((3, rows, features), bf16),
        pltpu.VMEM((rows, features), bf16),
        pltpu.VMEM((rows, tokens), bf16),
        pltpu.VMEM((ROWS, long_len), bf16),
        pltpu.VMEM((ROWS * plan.blocks, LANES), f32),
        pltpu.VMEM((ROWS * plan.blocks, LANES, LANES), bf16),
        pltpu.VMEM((3 * rows, tokens), f32),
        pltpu.VMEM((rows, tokens), f32),
        pltpu.VMEM((plan.plane, ROWS, LANES), f32),
        pltpu.VMEM((plan.ring, ROWS, LANES), f32),
        pltpu.VMEM((ROWS, LANES), f32),
        pltpu.VMEM((ctx, 2, ROWS, tokens), bf16),
        pltpu.VMEM((ctx, 2, ROWS, tokens), bf16),
        pltpu.VMEM((ctx, ROWS, tokens), bf16),
        pltpu.VMEM((ctx, ROWS, tokens), bf16),
        pltpu.VMEM((ctx, ROWS, tokens), bf16),
        pltpu.VMEM((ctx, ROWS, tokens), bf16),
        pltpu.VMEM((3, ROWS, LANES + long_len), f32),
        pltpu.VMEM((ROWS * 2 * plan.blocks, LANES), f32),
        pltpu.VMEM((ROWS * plan.blocks, LANES), f32),
        pltpu.VMEM((rows, LANES), f32),
        pltpu.VMEM((9, rows, LANES), f32),
        dma((4,)),
        dma((2, plan.plane)),
        dma((2, plan.ring)),
        *gather_sems,
        *gather_sems,
        dma((2, ctx)),
        dma((2, ctx)),
        dma((2, ctx)),
    ]
    return pl.pallas_call(
        functools.partial(kernel, plan),
        out_shape=jax.ShapeDtypeStruct((rows, tokens), bf16),
        in_specs=[anywhere, here, anywhere, here, anywhere, here, anywhere],
        out_specs=here,
        scratch_shapes=scratch,
        compiler_params=pltpu.CompilerParams(
            collective_id=0, has_side_effects=True, vmem_limit_bytes=56 * 1024 * 1024
        ),
        name="mixer",
    )(
        activations,
        norm_gain.reshape(1, rows),
        w_in,
        jnp.transpose(w_short, (0, 2, 1)),
        long_filter.reshape(groups, ROWS, long_len),
        skip_gain.reshape(1, rows),
        w_out,
    )


def solution(mesh):
    placed = (
        P("fsdp", "ctx"),
        P("fsdp"),
        P(None, "fsdp", None),
        P(None, "fsdp", None),
        P("fsdp", None),
        P("fsdp"),
        P("fsdp", None),
    )
    body = functools.partial(shards, mesh.shape["fsdp"], mesh.shape["ctx"])
    return jax.shard_map(body, mesh=mesh, in_specs=placed, out_specs=P("fsdp", "ctx"), check_vma=False)
```

```python
import functools

import jax
import jax.numpy as jnp
from jax import lax
from jax.experimental import pallas as pl
from jax.experimental.pallas import tpu as pltpu
from jax.sharding import PartitionSpec as P

EPSILON = 1e-05
MESH = pl.DeviceIdType.MESH
LANES = 128
ROWS = 8


class Plan:
    def __init__(self, fsdp, ctx, rows, tokens, long_len):
        self.cores = 2
        self.ring = {64: 8, 16: 4, 8: 4}[fsdp]
        self.line = fsdp // (self.ring * self.cores)
        self.plane = self.line * self.cores
        self.fsdp, self.ctx = fsdp, ctx
        self.rows, self.tokens, self.long_len = rows, tokens, long_len
        self.half = self.ring // 2
        self.blocks = long_len // LANES
        self.token_tiles = tokens // LANES


def copy_to(src, dst, send, recv, device):
    return pltpu.make_async_remote_copy(
        src_ref=src, dst_ref=dst, send_sem=send, recv_sem=recv, device_id=device, device_id_type=MESH
    )


def kernel(
    plan, act, gain, w_in, w_short, filt, skip, w_out, out,
    gath, mixg, win, wout, xin, hin, hrow, tmat, acc, acc2, plane_sum, ring_sum, scale,
    pbuf, rbuf, qbuf, qrecv, mbuf, mrecv, seq, gseq, fseq, skipb, tapb,
    lsem, plane_sem, ring_sem, zsem, ysem, lastsem, csem, zsem2, ysem2, lastsem2, csem2, asem, qsem, bsem,
):
    me = lax.axis_index("fsdp")
    ctx = lax.axis_index("ctx")
    ring, line, plane, half = plan.ring, plan.line, plan.plane, plan.half
    y = me // plane
    p = lax.rem(me, plane)
    z = p // plan.cores
    core = lax.rem(p, plan.cores)
    rows, tokens = plan.rows, plan.tokens

    def at(yy, zz, cc):
        return (yy * line + zz) * plan.cores + cc

    def turn(yy):
        return lax.rem(yy + 2 * ring, ring)

    loads = [
        pltpu.make_async_copy(act, xin, lsem.at[0]),
        pltpu.make_async_copy(filt.at[ctx], hin, lsem.at[1]),
        pltpu.make_async_copy(w_in, win, lsem.at[2]),
        pltpu.make_async_copy(w_out, wout, lsem.at[3]),
    ]
    loads[0].start()
    barrier = pltpu.get_barrier_semaphore()

    def greet(device):
        pl.semaphore_signal(barrier, inc=1, device_id=device, device_id_type=MESH)

    for o in [o for o in range(1, plan.ctx) if o % 2] + [o for o in range(2, plan.ctx, 2)]:
        greet({"ctx": ctx ^ o})

    @pl.loop(1, ring)
    def _(o):
        greet({"fsdp": turn(y + o) * plane + p})

    @pl.loop(1, plane)
    def _(o):
        greet({"fsdp": y * plane + (p ^ o)})

    for load in loads[1:]:
        load.start()

    def column(row):
        n = row.shape[1]
        same = lax.broadcasted_iota(jnp.int32, (n, n), 0) == lax.broadcasted_iota(jnp.int32, (n, n), 1)
        return jnp.sum(jnp.where(same, jnp.broadcast_to(row, (n, n)), 0.0), axis=1, keepdims=True)

    loads[0].wait()
    own = xin[...].astype(jnp.float32)
    gath[me] = (own * column(gain[...])).astype(jnp.bfloat16)
    squares = jnp.sum(own * own, axis=0, keepdims=True)
    plane_sum[0] = jnp.zeros((ROWS, LANES), jnp.float32)
    for k in range(plan.token_tiles):
        plane_sum[0, k : k + 1, :] = squares[:, k * LANES : (k + 1) * LANES]
    skipb[...] = jnp.broadcast_to(column(skip[...]), (rows, LANES))
    for k in range(9):
        tapb[k] = jnp.broadcast_to(column(w_short[k // 3, k % 3 : k % 3 + 1, :]), (rows, LANES))
    acc[...] = jnp.zeros_like(acc)
    acc2[...] = jnp.zeros_like(acc2)
    gseq[...] = jnp.zeros_like(gseq)
    seq[:, :, :LANES] = jnp.zeros((3, ROWS, LANES), jnp.float32)
    pl.semaphore_wait(barrier, (plane - 1) + (ring - 1) + (plan.ctx - 1))

    def plane_copy(o):
        return copy_to(
            plane_sum.at[0], plane_sum.at[o], plane_sem.at[0, o], plane_sem.at[1, o], {"fsdp": y * plane + (p ^ o)}
        )

    def ring_copy(o):
        return copy_to(
            ring_sum.at[0], ring_sum.at[o], ring_sem.at[0, o], ring_sem.at[1, o], {"fsdp": turn(y + o) * plane + p}
        )

    def gather(buf, zs, ys, bs, cs, multiply, fillers):
        first = rows - rows // 4
        last = ring - 1

        def place(r):
            if r < half:
                return turn(y - r)
            return turn(y + (r - half + 1)) if r < last else turn(y + half)

        def columns(s):
            return [s, half - 1 + s] if s < half else [last]

        def zcopy(o, zz_from):
            view = buf.at[at(y, zz_from, core), pl.ds(0, first)]
            return copy_to(view, view, zs.at[0, o], zs.at[1, o], {"fsdp": at(y, z ^ o, core)})

        def ycopy(r, o, yy, step, whole):
            block = at(yy, z ^ o, core)
            view = buf.at[block] if whole else buf.at[block, pl.ds(0, first)]
            return copy_to(view, view, ys.at[0, r, o], ys.at[1, r, o], {"fsdp": at(turn(y + step), z, core)})

        def bcopy(r, o, zz_from):
            view = buf.at[at(place(r), zz_from, core), pl.ds(first, rows - first)]
            return copy_to(view, view, bs.at[0, r, o], bs.at[1, r, o], {"fsdp": at(y, z ^ o, core)})

        def ccopy(r, o, cc):
            block = buf.at[at(place(r), z ^ o, cc)]
            return copy_to(block, block, cs.at[0, r, o], cs.at[1, r, o], {"fsdp": at(y, z, 1 - core)})

        def pass_on(d, s, o, whole):
            yy = turn(y - (s - 1)) if d == 0 else turn(y + (s - 1))
            copy = ycopy(columns(s)[d if s < half else 0], o, yy, 1 - 2 * d, whole)
            if s < half:
                copy.start()
            else:
                pl.when(core == d)(copy.start)

        def arrive(s, o):
            for d, r in enumerate(columns(s)):
                ycopy(r, o, place(r), 1, o == 0).wait_recv()
                if s < half:
                    pass_on(d, s + 1, o, o == 0)
                if o == 0:
                    spread_line(r)

        def spread_line(r):
            for k in range(1, line):
                bcopy(r, k, z).start()
            if r:
                ccopy(r, 0, core).start()

        def arrive_line(o):
            zcopy(o, z ^ o).wait_recv()
            for d in range(2):
                pass_on(d, 1, o, False)
            if o == 1:
                for k in range(3, line):
                    zcopy(k, z).start()
                spread_line(0)

        def hand_over(s, o):
            for r in columns(s) if s else [0]:
                bcopy(r, o, z ^ o).wait_recv()
                ccopy(r, o, core).start()

        def finish(s):
            for r in columns(s) if s else [0]:
                @pl.loop(0, line)
                def _(o):
                    ccopy(r, o, 1 - core).wait_recv()

                multiply(place(r))

        def drain(s):
            for r in columns(s) if s else [0]:
                if s:
                    ycopy(r, 0, y, 1, True).wait_send()
                ccopy(r, 0, core).wait_send()

                @pl.loop(1, line)
                def _(o):
                    if s:
                        ycopy(r, o, y, 1, False).wait_send()
                    else:
                        zcopy(o, z).wait_send()
                    bcopy(r, o, z).wait_send()
                    ccopy(r, o, core).wait_send()

        for d in range(2):
            pass_on(d, 1, 0, True)
        for o in range(1, min(line, 3)):
            zcopy(o, z).start()
        ccopy(0, 0, core).start()

        hop = 5.6
        crossed = [0.0] + [2.0 + 2.2 * o for o in range(1, line)]
        events = list(fillers)
        for o in range(1, line):
            events.append((crossed[o], functools.partial(arrive_line, o)))
        for s in range(half + 1):
            for o in range(line if s else 0):
                events.append((crossed[o] + hop * s, functools.partial(arrive, s, o)))
            for o in range(1, line):
                handed = max(crossed[o] + hop * s, hop * (s + 1)) + 0.1
                events.append((handed, functools.partial(hand_over, s, o)))
            handed = max(crossed[-1] + hop * s, hop * (s + 1)) + 0.1
            events.append((handed + 2.0, functools.partial(finish, s)))
            if s == half:
                events.append((handed + 1.0, functools.partial(drain, s - 1)))
            elif s < half - 1:
                events.append((handed + 10.0, functools.partial(drain, s)))
        for _, event in sorted(events, key=lambda e: e[0]):
            event()

        return functools.partial(drain, half)

    width = plane * rows

    def multiply_in(yy):
        w = win[:, :, pl.ds(pl.multiple_of(yy * width, width), width)].reshape(3 * rows, width)
        x = gath[pl.ds(yy * plane, plane)].reshape(width, tokens)
        acc[...] += jnp.dot(w, x, preferred_element_type=jnp.float32)

    def multiply_out(yy):
        w = wout[:, pl.ds(pl.multiple_of(yy * width, width), width)]
        x = mixg[pl.ds(yy * plane, plane)].reshape(width, tokens)
        acc2[...] += jnp.dot(w, x, preferred_element_type=jnp.float32)

    def spread_filter():
        for load in loads[1:]:
            load.wait()
        h = hin[...].astype(jnp.float32)
        for d in range(plan.blocks):
            hrow[pl.ds(d, ROWS, stride=plan.blocks), :] = h[:, d * LANES : (d + 1) * LANES]

    later = lax.broadcasted_iota(jnp.int32, (LANES, LANES), 1) >= lax.broadcasted_iota(jnp.int32, (LANES, LANES), 0)

    def band(first, last):
        @pl.loop(first, last)
        def _(c):
            def body(d, before):
                r = c * plan.blocks + d
                line_ = jnp.broadcast_to(hrow[pl.ds(r, 1), :], (LANES, LANES))
                rolled = pltpu.roll(line_, 0, 1, stride=1, stride_axis=0)
                tmat[r] = jnp.where(later, rolled, before).astype(jnp.bfloat16)
                return rolled

            lax.fori_loop(0, plan.blocks, body, jnp.zeros((LANES, LANES), jnp.float32), unroll=min(8, plan.blocks))

    def start_plane():
        @pl.loop(1, plane)
        def _(o):
            plane_copy(o).start()

    def start_ring():
        @pl.loop(1, plane)
        def _(o):
            plane_copy(o).wait_recv()

        ring_sum[0] = jnp.sum(plane_sum[...], axis=0)

        @pl.loop(1, ring)
        def _(o):
            ring_copy(o).start()

    def end_sum():
        @pl.loop(1, ring)
        def _(o):
            ring_copy(o).wait_recv()

        scale[...] = lax.rsqrt(jnp.sum(ring_sum[...], axis=0) / (plan.fsdp * rows) + EPSILON)

    fillers = [(21.0, end_sum), (0.0, start_plane), (4.3, spread_filter), (8.3, start_ring)]
    fillers += [(7.0 + 1.9 * i, functools.partial(band, i, i + 1)) for i in range(ROWS)]
    drain1 = gather(gath, zsem, ysem, lastsem, csem, multiply_in, fillers)

    factor = scale[...]

    def project(s, store):
        for k in range(plan.token_tiles):
            lanes = slice(k * LANES, (k + 1) * LANES)
            scaled = acc[s * rows : (s + 1) * rows, lanes] * factor[k : k + 1, :]
            for j in range(plan.ctx):
                store(j, lanes, scaled[j * ROWS : (j + 1) * ROWS].astype(jnp.bfloat16))

    def keep_key(j, lanes, value):
        pbuf[j, 0, :, lanes] = value

    def keep_value(j, lanes, value):
        pbuf[j, 1, :, lanes] = value

    def keep_query(j, lanes, value):
        qbuf[j, :, lanes] = value

    def swap(src, dst, sem):
        order = [o for o in range(1, plan.ctx) if o % 2] + [o for o in range(2, plan.ctx, 2)]

        def copy(o, slot):
            return copy_to(src.at[ctx ^ o], dst.at[slot], sem.at[0, o], sem.at[1, o], {"ctx": ctx ^ o})

        for o in order:
            copy(o, ctx).start()
        dst[ctx] = src[ctx]

        def arrive():
            for o in order:
                copy(o, ctx ^ o).wait_recv()

        def drain():
            for o in order:
                copy(o, ctx).wait_send()

        return arrive, drain

    project(1, keep_key)
    project(2, keep_value)
    arrive_gate, drain_gate = swap(pbuf, rbuf, asem)
    project(0, keep_query)
    arrive_query, drain_query = swap(qbuf, qrecv, qsem)

    @pl.loop(1, plane)
    def _(o):
        plane_copy(o).wait_send()

    @pl.loop(1, ring)
    def _(o):
        ring_copy(o).wait_send()

    drain1()
    arrive_gate()

    for j in range(plan.ctx):
        for s in range(2):
            seq[s + 1, :, LANES + j * tokens : LANES + (j + 1) * tokens] = rbuf[j, s].astype(jnp.float32)

    def smooth(s):
        taps = [tapb[3 * s + k, pl.ds(ctx * ROWS, ROWS), :][:, 0:1] for k in range(3)]
        full = seq[s]
        total = taps[0] * full + taps[1] * pltpu.roll(full, 1, 1)
        total = total + taps[2] * pltpu.roll(full, 2, 1)
        return total[:, LANES:]

    gated = (smooth(1) * smooth(2)).astype(jnp.bfloat16).astype(jnp.float32)
    blocks = plan.blocks
    for b in range(blocks):
        gseq[pl.ds(blocks + b, ROWS, stride=2 * blocks), :] = gated[:, b * LANES : (b + 1) * LANES]

    @pl.loop(0, ROWS, unroll=2)
    def _(c):
        base = c * 2 * blocks + blocks
        lhs = jnp.concatenate(
            [gseq[pl.ds(base - d, blocks), :].astype(jnp.bfloat16) for d in range(blocks)], axis=1
        )
        rhs = tmat[pl.ds(c * blocks, blocks)].reshape(blocks * LANES, LANES)
        fseq[pl.ds(c * blocks, blocks), :] = jnp.dot(lhs, rhs, preferred_element_type=jnp.float32)

    arrive_query()
    for j in range(plan.ctx):
        seq[0, :, LANES + j * tokens : LANES + (j + 1) * tokens] = qrecv[j].astype(jnp.float32)
    query = smooth(0)
    direct = skipb[pl.ds(ctx * ROWS, ROWS), :]
    for b in range(blocks):
        lanes = slice(b * LANES, (b + 1) * LANES)
        value = query[:, lanes] * (fseq[pl.ds(b, ROWS, stride=blocks), :] + direct * gated[:, lanes])
        j, k = b // plan.token_tiles, b % plan.token_tiles
        mbuf[j, :, k * LANES : (k + 1) * LANES] = value.astype(jnp.bfloat16)

    arrive_mixed, drain_mixed = swap(mbuf, mrecv, bsem)
    drain_gate()
    drain_query()
    arrive_mixed()
    mixg[me] = mrecv[...].astype(jnp.float32).reshape(rows, tokens).astype(jnp.bfloat16)

    drain4 = gather(mixg, zsem2, ysem2, lastsem2, csem2, multiply_out, [])
    out[...] = acc2[...].astype(jnp.bfloat16)
    drain_mixed()
    drain4()


def shards(fsdp, ctx, activations, norm_gain, w_in, w_short, long_filter, skip_gain, w_out):
    rows, tokens = activations.shape
    long_len = long_filter.shape[1]
    plan = Plan(fsdp, ctx, rows, tokens, long_len)
    groups = rows // ROWS
    features = fsdp * rows
    bf16, f32 = jnp.bfloat16, jnp.float32
    dma = pltpu.SemaphoreType.DMA
    anywhere = pl.BlockSpec(memory_space=pl.ANY)
    here = pl.BlockSpec(memory_space=pltpu.VMEM)
    gather_sems = [
        dma((2, max(plan.line, 2))),
        dma((2, plan.ring, plan.line)),
        dma((2, plan.ring, max(plan.line, 2))),
        dma((2, plan.ring, plan.line)),
    ]
    scratch = [
        pltpu.VMEM((fsdp, rows, tokens), bf16),
        pltpu.VMEM((fsdp, rows, tokens), bf16),
        pltpu.VMEM((3, rows, features), bf16),
        pltpu.VMEM((rows, features), bf16),
        pltpu.VMEM((rows, tokens), bf16),
        pltpu.VMEM((ROWS, long_len), bf16),
        pltpu.VMEM((ROWS * plan.blocks, LANES), f32),
        pltpu.VMEM((ROWS * plan.blocks, LANES, LANES), bf16),
        pltpu.VMEM((3 * rows, tokens), f32),
        pltpu.VMEM((rows, tokens), f32),
        pltpu.VMEM((plan.plane, ROWS, LANES), f32),
        pltpu.VMEM((plan.ring, ROWS, LANES), f32),
        pltpu.VMEM((ROWS, LANES), f32),
        pltpu.VMEM((ctx, 2, ROWS, tokens), bf16),
        pltpu.VMEM((ctx, 2, ROWS, tokens), bf16),
        pltpu.VMEM((ctx, ROWS, tokens), bf16),
        pltpu.VMEM((ctx, ROWS, tokens), bf16),
        pltpu.VMEM((ctx, ROWS, tokens), bf16),
        pltpu.VMEM((ctx, ROWS, tokens), bf16),
        pltpu.VMEM((3, ROWS, LANES + long_len), f32),
        pltpu.VMEM((ROWS * 2 * plan.blocks, LANES), f32),
        pltpu.VMEM((ROWS * plan.blocks, LANES), f32),
        pltpu.VMEM((rows, LANES), f32),
        pltpu.VMEM((9, rows, LANES), f32),
        dma((4,)),
        dma((2, plan.plane)),
        dma((2, plan.ring)),
        *gather_sems,
        *gather_sems,
        dma((2, ctx)),
        dma((2, ctx)),
        dma((2, ctx)),
    ]
    return pl.pallas_call(
        functools.partial(kernel, plan),
        out_shape=jax.ShapeDtypeStruct((rows, tokens), bf16),
        in_specs=[anywhere, here, anywhere, here, anywhere, here, anywhere],
        out_specs=here,
        scratch_shapes=scratch,
        compiler_params=pltpu.CompilerParams(
            collective_id=0, has_side_effects=True, vmem_limit_bytes=56 * 1024 * 1024
        ),
        name="mixer",
    )(
        activations,
        norm_gain.reshape(1, rows),
        w_in,
        jnp.transpose(w_short, (0, 2, 1)),
        long_filter.reshape(groups, ROWS, long_len),
        skip_gain.reshape(1, rows),
        w_out,
    )


def solution(mesh):
    placed = (
        P("fsdp", "ctx"),
        P("fsdp"),
        P(None, "fsdp", None),
        P(None, "fsdp", None),
        P("fsdp", None),
        P("fsdp"),
        P("fsdp", None),
    )
    body = functools.partial(shards, mesh.shape["fsdp"], mesh.shape["ctx"])
    return jax.shard_map(body, mesh=mesh, in_specs=placed, out_specs=P("fsdp", "ctx"), check_vma=False)
```

```python
import functools

import jax
import jax.numpy as jnp
from jax import lax
from jax.experimental import pallas as pl
from jax.experimental.pallas import tpu as pltpu
from jax.sharding import PartitionSpec as P

EPSILON = 1e-05
MESH = pl.DeviceIdType.MESH
LANES = 128
ROWS = 8


class Plan:
    def __init__(self, fsdp, ctx, rows, tokens, long_len):
        self.cores = 2
        self.ring = {64: 8, 16: 4, 8: 4}[fsdp]
        self.line = fsdp // (self.ring * self.cores)
        self.plane = self.line * self.cores
        self.fsdp, self.ctx = fsdp, ctx
        self.rows, self.tokens, self.long_len = rows, tokens, long_len
        self.half = self.ring // 2
        self.blocks = long_len // LANES
        self.token_tiles = tokens // LANES


def copy_to(src, dst, send, recv, device):
    return pltpu.make_async_remote_copy(
        src_ref=src, dst_ref=dst, send_sem=send, recv_sem=recv, device_id=device, device_id_type=MESH
    )


def kernel(
    plan, act, gain, w_in, w_short, filt, skip, w_out, out,
    gath, mixg, win, wout, xin, hin, hrow, tmat, acc, acc2, plane_sum, ring_sum, scale,
    pbuf, rbuf, qbuf, qrecv, mbuf, mrecv, seq, gseq, fseq, skipb, tapb,
    lsem, plane_sem, ring_sem, zsem, ysem, lastsem, csem, zsem2, ysem2, lastsem2, csem2, asem, qsem, bsem,
):
    me = lax.axis_index("fsdp")
    ctx = lax.axis_index("ctx")
    ring, line, plane, half = plan.ring, plan.line, plan.plane, plan.half
    y = me // plane
    p = lax.rem(me, plane)
    z = p // plan.cores
    core = lax.rem(p, plan.cores)
    rows, tokens = plan.rows, plan.tokens

    def at(yy, zz, cc):
        return (yy * line + zz) * plan.cores + cc

    def turn(yy):
        return lax.rem(yy + 2 * ring, ring)

    loads = [
        pltpu.make_async_copy(act, xin, lsem.at[0]),
        pltpu.make_async_copy(filt.at[ctx], hin, lsem.at[1]),
        pltpu.make_async_copy(w_in, win, lsem.at[2]),
        pltpu.make_async_copy(w_out, wout, lsem.at[3]),
    ]
    loads[0].start()
    barrier = pltpu.get_barrier_semaphore()

    def greet(device):
        pl.semaphore_signal(barrier, inc=1, device_id=device, device_id_type=MESH)

    for o in [o for o in range(1, plan.ctx) if o % 2] + [o for o in range(2, plan.ctx, 2)]:
        greet({"ctx": ctx ^ o})

    @pl.loop(1, ring)
    def _(o):
        greet({"fsdp": turn(y + o) * plane + p})

    @pl.loop(1, plane)
    def _(o):
        greet({"fsdp": y * plane + (p ^ o)})

    for load in loads[1:]:
        load.start()

    def column(row):
        n = row.shape[1]
        same = lax.broadcasted_iota(jnp.int32, (n, n), 0) == lax.broadcasted_iota(jnp.int32, (n, n), 1)
        return jnp.sum(jnp.where(same, jnp.broadcast_to(row, (n, n)), 0.0), axis=1, keepdims=True)

    loads[0].wait()
    own = xin[...].astype(jnp.float32)
    gath[me] = (own * column(gain[...])).astype(jnp.bfloat16)
    squares = jnp.sum(own * own, axis=0, keepdims=True)
    plane_sum[0] = jnp.zeros((ROWS, LANES), jnp.float32)
    for k in range(plan.token_tiles):
        plane_sum[0, k : k + 1, :] = squares[:, k * LANES : (k + 1) * LANES]
    skipb[...] = jnp.broadcast_to(column(skip[...]), (rows, LANES))
    for k in range(9):
        tapb[k] = jnp.broadcast_to(column(w_short[k // 3, k % 3 : k % 3 + 1, :]), (rows, LANES))
    acc[...] = jnp.zeros_like(acc)
    acc2[...] = jnp.zeros_like(acc2)
    gseq[...] = jnp.zeros_like(gseq)
    seq[:, :, :LANES] = jnp.zeros((3, ROWS, LANES), jnp.float32)
    pl.semaphore_wait(barrier, (plane - 1) + (ring - 1) + (plan.ctx - 1))

    def plane_copy(o):
        return copy_to(
            plane_sum.at[0], plane_sum.at[o], plane_sem.at[0, o], plane_sem.at[1, o], {"fsdp": y * plane + (p ^ o)}
        )

    def ring_copy(o):
        return copy_to(
            ring_sum.at[0], ring_sum.at[o], ring_sem.at[0, o], ring_sem.at[1, o], {"fsdp": turn(y + o) * plane + p}
        )

    def gather(buf, zs, ys, bs, cs, multiply, fillers):
        first = rows - rows // 4
        last = ring - 1

        def place(r):
            if r < half:
                return turn(y - r)
            return turn(y + (r - half + 1)) if r < last else turn(y + half)

        def columns(s):
            return [s, half - 1 + s] if s < half else [last]

        def zcopy(o, zz_from):
            view = buf.at[at(y, zz_from, core), pl.ds(0, first)]
            return copy_to(view, view, zs.at[0, o], zs.at[1, o], {"fsdp": at(y, z ^ o, core)})

        def ycopy(r, o, yy, step, whole):
            block = at(yy, z ^ o, core)
            view = buf.at[block] if whole else buf.at[block, pl.ds(0, first)]
            return copy_to(view, view, ys.at[0, r, o], ys.at[1, r, o], {"fsdp": at(turn(y + step), z, core)})

        def bcopy(r, o, zz_from):
            view = buf.at[at(place(r), zz_from, core), pl.ds(first, rows - first)]
            return copy_to(view, view, bs.at[0, r, o], bs.at[1, r, o], {"fsdp": at(y, z ^ o, core)})

        def ccopy(r, o, cc):
            block = buf.at[at(place(r), z ^ o, cc)]
            return copy_to(block, block, cs.at[0, r, o], cs.at[1, r, o], {"fsdp": at(y, z, 1 - core)})

        def pass_on(d, s, o, whole):
            yy = turn(y - (s - 1)) if d == 0 else turn(y + (s - 1))
            copy = ycopy(columns(s)[d if s < half else 0], o, yy, 1 - 2 * d, whole)
            if s < half:
                copy.start()
            else:
                pl.when(core == d)(copy.start)

        def arrive(s, o):
            for d, r in enumerate(columns(s)):
                ycopy(r, o, place(r), 1, o == 0).wait_recv()
                if s < half:
                    pass_on(d, s + 1, o, o == 0)
                if o == 0:
                    spread_line(r)

        def spread_line(r):
            for k in range(1, line):
                bcopy(r, k, z).start()
            if r:
                ccopy(r, 0, core).start()

        def arrive_line(o):
            zcopy(o, z ^ o).wait_recv()
            for d in range(2):
                pass_on(d, 1, o, False)
            if o == 1:
                spread_line(0)

        def hand_over(s, o):
            for r in columns(s) if s else [0]:
                bcopy(r, o, z ^ o).wait_recv()
                ccopy(r, o, core).start()

        def finish(s):
            for r in columns(s) if s else [0]:
                @pl.loop(0, line)
                def _(o):
                    ccopy(r, o, 1 - core).wait_recv()

                multiply(place(r))

        def drain(s):
            for r in columns(s) if s else [0]:
                if s:
                    ycopy(r, 0, y, 1, True).wait_send()
                ccopy(r, 0, core).wait_send()

                @pl.loop(1, line)
                def _(o):
                    if s:
                        ycopy(r, o, y, 1, False).wait_send()
                    else:
                        zcopy(o, z).wait_send()
                    bcopy(r, o, z).wait_send()
                    ccopy(r, o, core).wait_send()

        for o in reversed(range(1, line)):
            zcopy(o, z).start()
        for d in range(2):
            pass_on(d, 1, 0, True)
        ccopy(0, 0, core).start()

        hop = 5.6
        crossed = [0.0] + [2.0 + 2.2 * o for o in range(1, line)]
        events = list(fillers)
        for o in range(1, line):
            events.append((crossed[o], functools.partial(arrive_line, o)))
        for s in range(half + 1):
            for o in range(line if s else 0):
                events.append((crossed[o] + hop * s, functools.partial(arrive, s, o)))
            for o in range(1, line):
                handed = max(crossed[o] + hop * s, hop * (s + 1)) + 0.1
                events.append((handed, functools.partial(hand_over, s, o)))
            handed = max(crossed[-1] + hop * s, hop * (s + 1)) + 0.1
            events.append((handed + 2.0, functools.partial(finish, s)))
            if s == half:
                events.append((handed + 1.0, functools.partial(drain, s - 1)))
            elif s < half - 1:
                events.append((handed + 10.0, functools.partial(drain, s)))
        for _, event in sorted(events, key=lambda e: e[0]):
            event()

        return functools.partial(drain, half)

    width = plane * rows

    def multiply_in(yy):
        w = win[:, :, pl.ds(pl.multiple_of(yy * width, width), width)].reshape(3 * rows, width)
        x = gath[pl.ds(yy * plane, plane)].reshape(width, tokens)
        acc[...] += jnp.dot(w, x, preferred_element_type=jnp.float32)

    def multiply_out(yy):
        w = wout[:, pl.ds(pl.multiple_of(yy * width, width), width)]
        x = mixg[pl.ds(yy * plane, plane)].reshape(width, tokens)
        acc2[...] += jnp.dot(w, x, preferred_element_type=jnp.float32)

    def spread_filter():
        for load in loads[1:]:
            load.wait()
        h = hin[...].astype(jnp.float32)
        for d in range(plan.blocks):
            hrow[pl.ds(d, ROWS, stride=plan.blocks), :] = h[:, d * LANES : (d + 1) * LANES]

    later = lax.broadcasted_iota(jnp.int32, (LANES, LANES), 1) >= lax.broadcasted_iota(jnp.int32, (LANES, LANES), 0)

    def band(first, last):
        @pl.loop(first, last)
        def _(c):
            def body(d, before):
                r = c * plan.blocks + d
                line_ = jnp.broadcast_to(hrow[pl.ds(r, 1), :], (LANES, LANES))
                rolled = pltpu.roll(line_, 0, 1, stride=1, stride_axis=0)
                tmat[r] = jnp.where(later, rolled, before).astype(jnp.bfloat16)
                return rolled

            lax.fori_loop(0, plan.blocks, body, jnp.zeros((LANES, LANES), jnp.float32), unroll=min(8, plan.blocks))

    def start_plane():
        @pl.loop(1, plane)
        def _(o):
            plane_copy(o).start()

    def start_ring():
        @pl.loop(1, plane)
        def _(o):
            plane_copy(o).wait_recv()

        ring_sum[0] = jnp.sum(plane_sum[...], axis=0)

        @pl.loop(1, ring)
        def _(o):
            ring_copy(o).start()

    def end_sum():
        @pl.loop(1, ring)
        def _(o):
            ring_copy(o).wait_recv()

        scale[...] = lax.rsqrt(jnp.sum(ring_sum[...], axis=0) / (plan.fsdp * rows) + EPSILON)

    fillers = [(21.0, end_sum), (0.0, start_plane), (4.3, spread_filter), (8.3, start_ring)]
    fillers += [(7.0 + 1.9 * i, functools.partial(band, i, i + 1)) for i in range(ROWS)]
    drain1 = gather(gath, zsem, ysem, lastsem, csem, multiply_in, fillers)

    factor = scale[...]

    def project(s, store):
        for k in range(plan.token_tiles):
            lanes = slice(k * LANES, (k + 1) * LANES)
            scaled = acc[s * rows : (s + 1) * rows, lanes] * factor[k : k + 1, :]
            for j in range(plan.ctx):
                store(j, lanes, scaled[j * ROWS : (j + 1) * ROWS].astype(jnp.bfloat16))

    def keep_key(j, lanes, value):
        pbuf[j, 0, :, lanes] = value

    def keep_value(j, lanes, value):
        pbuf[j, 1, :, lanes] = value

    def keep_query(j, lanes, value):
        qbuf[j, :, lanes] = value

    def swap(src, dst, sem):
        order = [o for o in range(1, plan.ctx) if o % 2] + [o for o in range(2, plan.ctx, 2)]

        def copy(o, slot):
            return copy_to(src.at[ctx ^ o], dst.at[slot], sem.at[0, o], sem.at[1, o], {"ctx": ctx ^ o})

        for o in order:
            copy(o, ctx).start()
        dst[ctx] = src[ctx]

        def arrive():
            for o in order:
                copy(o, ctx ^ o).wait_recv()

        def drain():
            for o in order:
                copy(o, ctx).wait_send()

        return arrive, drain

    project(1, keep_key)
    project(2, keep_value)
    arrive_gate, drain_gate = swap(pbuf, rbuf, asem)
    project(0, keep_query)
    arrive_query, drain_query = swap(qbuf, qrecv, qsem)

    @pl.loop(1, plane)
    def _(o):
        plane_copy(o).wait_send()

    @pl.loop(1, ring)
    def _(o):
        ring_copy(o).wait_send()

    drain1()
    arrive_gate()

    for j in range(plan.ctx):
        for s in range(2):
            seq[s + 1, :, LANES + j * tokens : LANES + (j + 1) * tokens] = rbuf[j, s].astype(jnp.float32)

    def smooth(s):
        taps = [tapb[3 * s + k, pl.ds(ctx * ROWS, ROWS), :][:, 0:1] for k in range(3)]
        full = seq[s]
        total = taps[0] * full + taps[1] * pltpu.roll(full, 1, 1)
        total = total + taps[2] * pltpu.roll(full, 2, 1)
        return total[:, LANES:]

    gated = (smooth(1) * smooth(2)).astype(jnp.bfloat16).astype(jnp.float32)
    blocks = plan.blocks
    for b in range(blocks):
        gseq[pl.ds(blocks + b, ROWS, stride=2 * blocks), :] = gated[:, b * LANES : (b + 1) * LANES]

    @pl.loop(0, ROWS, unroll=2)
    def _(c):
        base = c * 2 * blocks + blocks
        lhs = jnp.concatenate(
            [gseq[pl.ds(base - d, blocks), :].astype(jnp.bfloat16) for d in range(blocks)], axis=1
        )
        rhs = tmat[pl.ds(c * blocks, blocks)].reshape(blocks * LANES, LANES)
        fseq[pl.ds(c * blocks, blocks), :] = jnp.dot(lhs, rhs, preferred_element_type=jnp.float32)

    arrive_query()
    for j in range(plan.ctx):
        seq[0, :, LANES + j * tokens : LANES + (j + 1) * tokens] = qrecv[j].astype(jnp.float32)
    query = smooth(0)
    direct = skipb[pl.ds(ctx * ROWS, ROWS), :]
    for b in range(blocks):
        lanes = slice(b * LANES, (b + 1) * LANES)
        value = query[:, lanes] * (fseq[pl.ds(b, ROWS, stride=blocks), :] + direct * gated[:, lanes])
        j, k = b // plan.token_tiles, b % plan.token_tiles
        mbuf[j, :, k * LANES : (k + 1) * LANES] = value.astype(jnp.bfloat16)

    arrive_mixed, drain_mixed = swap(mbuf, mrecv, bsem)
    drain_gate()
    drain_query()
    arrive_mixed()
    mixg[me] = mrecv[...].astype(jnp.float32).reshape(rows, tokens).astype(jnp.bfloat16)

    drain4 = gather(mixg, zsem2, ysem2, lastsem2, csem2, multiply_out, [])
    out[...] = acc2[...].astype(jnp.bfloat16)
    drain_mixed()
    drain4()


def shards(fsdp, ctx, activations, norm_gain, w_in, w_short, long_filter, skip_gain, w_out):
    rows, tokens = activations.shape
    long_len = long_filter.shape[1]
    plan = Plan(fsdp, ctx, rows, tokens, long_len)
    groups = rows // ROWS
    features = fsdp * rows
    bf16, f32 = jnp.bfloat16, jnp.float32
    dma = pltpu.SemaphoreType.DMA
    anywhere = pl.BlockSpec(memory_space=pl.ANY)
    here = pl.BlockSpec(memory_space=pltpu.VMEM)
    gather_sems = [
        dma((2, max(plan.line, 2))),
        dma((2, plan.ring, plan.line)),
        dma((2, plan.ring, max(plan.line, 2))),
        dma((2, plan.ring, plan.line)),
    ]
    scratch = [
        pltpu.VMEM((fsdp, rows, tokens), bf16),
        pltpu.VMEM((fsdp, rows, tokens), bf16),
        pltpu.VMEM((3, rows, features), bf16),
        pltpu.VMEM((rows, features), bf16),
        pltpu.VMEM((rows, tokens), bf16),
        pltpu.VMEM((ROWS, long_len), bf16),
        pltpu.VMEM((ROWS * plan.blocks, LANES), f32),
        pltpu.VMEM((ROWS * plan.blocks, LANES, LANES), bf16),
        pltpu.VMEM((3 * rows, tokens), f32),
        pltpu.VMEM((rows, tokens), f32),
        pltpu.VMEM((plan.plane, ROWS, LANES), f32),
        pltpu.VMEM((plan.ring, ROWS, LANES), f32),
        pltpu.VMEM((ROWS, LANES), f32),
        pltpu.VMEM((ctx, 2, ROWS, tokens), bf16),
        pltpu.VMEM((ctx, 2, ROWS, tokens), bf16),
        pltpu.VMEM((ctx, ROWS, tokens), bf16),
        pltpu.VMEM((ctx, ROWS, tokens), bf16),
        pltpu.VMEM((ctx, ROWS, tokens), bf16),
        pltpu.VMEM((ctx, ROWS, tokens), bf16),
        pltpu.VMEM((3, ROWS, LANES + long_len), f32),
        pltpu.VMEM((ROWS * 2 * plan.blocks, LANES), f32),
        pltpu.VMEM((ROWS * plan.blocks, LANES), f32),
        pltpu.VMEM((rows, LANES), f32),
        pltpu.VMEM((9, rows, LANES), f32),
        dma((4,)),
        dma((2, plan.plane)),
        dma((2, plan.ring)),
        *gather_sems,
        *gather_sems,
        dma((2, ctx)),
        dma((2, ctx)),
        dma((2, ctx)),
    ]
    return pl.pallas_call(
        functools.partial(kernel, plan),
        out_shape=jax.ShapeDtypeStruct((rows, tokens), bf16),
        in_specs=[anywhere, here, anywhere, here, anywhere, here, anywhere],
        out_specs=here,
        scratch_shapes=scratch,
        compiler_params=pltpu.CompilerParams(
            collective_id=0, has_side_effects=True, vmem_limit_bytes=56 * 1024 * 1024
        ),
        name="mixer",
    )(
        activations,
        norm_gain.reshape(1, rows),
        w_in,
        jnp.transpose(w_short, (0, 2, 1)),
        long_filter.reshape(groups, ROWS, long_len),
        skip_gain.reshape(1, rows),
        w_out,
    )


def solution(mesh):
    placed = (
        P("fsdp", "ctx"),
        P("fsdp"),
        P(None, "fsdp", None),
        P(None, "fsdp", None),
        P("fsdp", None),
        P("fsdp"),
        P("fsdp", None),
    )
    body = functools.partial(shards, mesh.shape["fsdp"], mesh.shape["ctx"])
    return jax.shard_map(body, mesh=mesh, in_specs=placed, out_specs=P("fsdp", "ctx"), check_vma=False)
```

```python
import functools

import jax
import jax.numpy as jnp
from jax import lax
from jax.experimental import pallas as pl
from jax.experimental.pallas import tpu as pltpu
from jax.sharding import PartitionSpec as P

EPSILON = 1e-05
MESH = pl.DeviceIdType.MESH
LANES = 128
ROWS = 8


class Plan:
    def __init__(self, fsdp, ctx, rows, tokens, long_len):
        self.cores = 2
        self.ring = {64: 8, 16: 4, 8: 4}[fsdp]
        self.line = fsdp // (self.ring * self.cores)
        self.plane = self.line * self.cores
        self.fsdp, self.ctx = fsdp, ctx
        self.rows, self.tokens, self.long_len = rows, tokens, long_len
        self.half = self.ring // 2
        self.blocks = long_len // LANES
        self.token_tiles = tokens // LANES


def copy_to(src, dst, send, recv, device):
    return pltpu.make_async_remote_copy(
        src_ref=src, dst_ref=dst, send_sem=send, recv_sem=recv, device_id=device, device_id_type=MESH
    )


def kernel(
    plan, act, gain, w_in, w_short, filt, skip, w_out, out,
    gath, mixg, win, wout, xin, hin, hrow, tmat, acc, acc2, plane_sum, ring_sum, scale,
    pbuf, rbuf, qbuf, qrecv, mbuf, mrecv, seq, gseq, fseq, skipb, tapb,
    lsem, plane_sem, ring_sem, zsem, ysem, lastsem, csem, zsem2, ysem2, lastsem2, csem2, asem, qsem, bsem,
):
    me = lax.axis_index("fsdp")
    ctx = lax.axis_index("ctx")
    ring, line, plane, half = plan.ring, plan.line, plan.plane, plan.half
    y = me // plane
    p = lax.rem(me, plane)
    z = p // plan.cores
    core = lax.rem(p, plan.cores)
    rows, tokens = plan.rows, plan.tokens

    def at(yy, zz, cc):
        return (yy * line + zz) * plan.cores + cc

    def turn(yy):
        return lax.rem(yy + 2 * ring, ring)

    loads = [
        pltpu.make_async_copy(act, xin, lsem.at[0]),
        pltpu.make_async_copy(filt.at[ctx], hin, lsem.at[1]),
        pltpu.make_async_copy(w_in, win, lsem.at[2]),
        pltpu.make_async_copy(w_out, wout, lsem.at[3]),
    ]
    loads[0].start()
    barrier = pltpu.get_barrier_semaphore()

    def greet(device):
        pl.semaphore_signal(barrier, inc=1, device_id=device, device_id_type=MESH)

    for o in [o for o in range(1, plan.ctx) if o % 2] + [o for o in range(2, plan.ctx, 2)]:
        greet({"ctx": ctx ^ o})

    @pl.loop(1, ring)
    def _(o):
        greet({"fsdp": turn(y + o) * plane + p})

    @pl.loop(1, plane)
    def _(o):
        greet({"fsdp": y * plane + (p ^ o)})

    for load in loads[1:]:
        load.start()

    def column(row):
        n = row.shape[1]
        same = lax.broadcasted_iota(jnp.int32, (n, n), 0) == lax.broadcasted_iota(jnp.int32, (n, n), 1)
        return jnp.sum(jnp.where(same, jnp.broadcast_to(row, (n, n)), 0.0), axis=1, keepdims=True)

    loads[0].wait()
    own = xin[...].astype(jnp.float32)
    gath[me] = (own * column(gain[...])).astype(jnp.bfloat16)
    squares = jnp.sum(own * own, axis=0, keepdims=True)
    plane_sum[0] = jnp.zeros((ROWS, LANES), jnp.float32)
    for k in range(plan.token_tiles):
        plane_sum[0, k : k + 1, :] = squares[:, k * LANES : (k + 1) * LANES]
    skipb[...] = jnp.broadcast_to(column(skip[...]), (rows, LANES))
    for k in range(9):
        tapb[k] = jnp.broadcast_to(column(w_short[k // 3, k % 3 : k % 3 + 1, :]), (rows, LANES))
    acc[...] = jnp.zeros_like(acc)
    acc2[...] = jnp.zeros_like(acc2)
    gseq[...] = jnp.zeros_like(gseq)
    seq[:, :, :LANES] = jnp.zeros((3, ROWS, LANES), jnp.float32)
    pl.semaphore_wait(barrier, (plane - 1) + (ring - 1) + (plan.ctx - 1))

    def plane_copy(o):
        return copy_to(
            plane_sum.at[0], plane_sum.at[o], plane_sem.at[0, o], plane_sem.at[1, o], {"fsdp": y * plane + (p ^ o)}
        )

    def ring_copy(o):
        return copy_to(
            ring_sum.at[0], ring_sum.at[o], ring_sem.at[0, o], ring_sem.at[1, o], {"fsdp": turn(y + o) * plane + p}
        )

    def gather(buf, zs, ys, bs, cs, multiply, fillers):
        first = rows - rows // 4
        last = ring - 1

        def place(r):
            if r < half:
                return turn(y - r)
            return turn(y + (r - half + 1)) if r < last else turn(y + half)

        def columns(s):
            return [s, half - 1 + s] if s < half else [last]

        def zcopy(o, zz_from):
            view = buf.at[at(y, zz_from, core), pl.ds(0, first)]
            return copy_to(view, view, zs.at[0, o], zs.at[1, o], {"fsdp": at(y, z ^ o, core)})

        def ycopy(r, o, yy, step, whole):
            block = at(yy, z ^ o, core)
            view = buf.at[block] if whole else buf.at[block, pl.ds(0, first)]
            return copy_to(view, view, ys.at[0, r, o], ys.at[1, r, o], {"fsdp": at(turn(y + step), z, core)})

        def bcopy(r, o, zz_from):
            view = buf.at[at(place(r), zz_from, core), pl.ds(first, rows - first)]
            return copy_to(view, view, bs.at[0, r, o], bs.at[1, r, o], {"fsdp": at(y, z ^ o, core)})

        def ccopy(r, o, cc):
            block = buf.at[at(place(r), z ^ o, cc)]
            return copy_to(block, block, cs.at[0, r, o], cs.at[1, r, o], {"fsdp": at(y, z, 1 - core)})

        def pass_on(d, s, o, whole):
            yy = turn(y - (s - 1)) if d == 0 else turn(y + (s - 1))
            copy = ycopy(columns(s)[d if s < half else 0], o, yy, 1 - 2 * d, whole)
            if s < half:
                copy.start()
            else:
                pl.when(core == d)(copy.start)

        def arrive(s, o):
            for d, r in enumerate(columns(s)):
                ycopy(r, o, place(r), 1, o == 0).wait_recv()
                if s < half:
                    pass_on(d, s + 1, o, o == 0)
                if o == 0:
                    spread_line(r)

        def spread_line(r):
            for k in range(1, line):
                bcopy(r, k, z).start()
            if r:
                ccopy(r, 0, core).start()

        def arrive_line(o):
            zcopy(o, z ^ o).wait_recv()
            for d in range(2):
                pass_on(d, 1, o, False)
            if o == 1:
                spread_line(0)

        def hand_over(s, o):
            for r in columns(s) if s else [0]:
                bcopy(r, o, z ^ o).wait_recv()
                ccopy(r, o, core).start()

        def finish(s):
            for r in columns(s) if s else [0]:
                @pl.loop(0, line)
                def _(o):
                    ccopy(r, o, 1 - core).wait_recv()

                multiply(place(r))

        def drain(s):
            for r in columns(s) if s else [0]:
                if s:
                    ycopy(r, 0, y, 1, True).wait_send()
                ccopy(r, 0, core).wait_send()

                @pl.loop(1, line)
                def _(o):
                    if s:
                        ycopy(r, o, y, 1, False).wait_send()
                    else:
                        zcopy(o, z).wait_send()
                    bcopy(r, o, z).wait_send()
                    ccopy(r, o, core).wait_send()

        for d in range(2):
            pass_on(d, 1, 0, True)
        for o in range(1, line):
            zcopy(o, z).start()
        ccopy(0, 0, core).start()

        hop = 5.6
        crossed = [0.0] + [2.0 + 2.2 * o for o in range(1, line)]
        events = list(fillers)
        for o in range(1, line):
            events.append((crossed[o], functools.partial(arrive_line, o)))
        for s in range(half + 1):
            for o in range(line if s else 0):
                events.append((crossed[o] + hop * s, functools.partial(arrive, s, o)))
            for o in range(1, line):
                handed = max(crossed[o] + hop * s, hop * (s + 1)) + 0.1
                events.append((handed, functools.partial(hand_over, s, o)))
            handed = max(crossed[-1] + hop * s, hop * (s + 1)) + 0.1
            events.append((handed + 2.0, functools.partial(finish, s)))
            if s == half:
                events.append((handed + 1.0, functools.partial(drain, s - 1)))
            elif s < half - 1:
                events.append((handed + 10.0, functools.partial(drain, s)))
        for _, event in sorted(events, key=lambda e: e[0]):
            event()

        return functools.partial(drain, half)

    width = plane * rows

    def multiply_in(yy):
        w = win[:, :, pl.ds(pl.multiple_of(yy * width, width), width)].reshape(3 * rows, width)
        x = gath[pl.ds(yy * plane, plane)].reshape(width, tokens)
        acc[...] += jnp.dot(w, x, preferred_element_type=jnp.float32)

    def multiply_out(yy):
        w = wout[:, pl.ds(pl.multiple_of(yy * width, width), width)]
        x = mixg[pl.ds(yy * plane, plane)].reshape(width, tokens)
        acc2[...] += jnp.dot(w, x, preferred_element_type=jnp.float32)

    def spread_filter():
        for load in loads[1:]:
            load.wait()
        h = hin[...].astype(jnp.float32)
        for d in range(plan.blocks):
            hrow[pl.ds(d, ROWS, stride=plan.blocks), :] = h[:, d * LANES : (d + 1) * LANES]

    later = lax.broadcasted_iota(jnp.int32, (LANES, LANES), 1) >= lax.broadcasted_iota(jnp.int32, (LANES, LANES), 0)

    def band(first, last):
        @pl.loop(first, last)
        def _(c):
            def body(d, before):
                r = c * plan.blocks + d
                line_ = jnp.broadcast_to(hrow[pl.ds(r, 1), :], (LANES, LANES))
                rolled = pltpu.roll(line_, 0, 1, stride=1, stride_axis=0)
                tmat[r] = jnp.where(later, rolled, before).astype(jnp.bfloat16)
                return rolled

            lax.fori_loop(0, plan.blocks, body, jnp.zeros((LANES, LANES), jnp.float32), unroll=min(8, plan.blocks))

    def start_plane():
        @pl.loop(1, plane)
        def _(o):
            plane_copy(o).start()

    def start_ring():
        @pl.loop(1, plane)
        def _(o):
            plane_copy(o).wait_recv()

        ring_sum[0] = jnp.sum(plane_sum[...], axis=0)

        @pl.loop(1, ring)
        def _(o):
            ring_copy(o).start()

    def end_sum():
        @pl.loop(1, ring)
        def _(o):
            ring_copy(o).wait_recv()

        scale[...] = lax.rsqrt(jnp.sum(ring_sum[...], axis=0) / (plan.fsdp * rows) + EPSILON)

    fillers = [(21.0, end_sum), (0.0, start_plane), (4.3, spread_filter), (8.3, start_ring)]
    fillers += [(7.0 + 1.9 * i, functools.partial(band, i, i + 1)) for i in range(ROWS)]
    drain1 = gather(gath, zsem, ysem, lastsem, csem, multiply_in, fillers)

    factor = scale[...]

    def project(s, store):
        for k in range(plan.token_tiles):
            lanes = slice(k * LANES, (k + 1) * LANES)
            scaled = acc[s * rows : (s + 1) * rows, lanes] * factor[k : k + 1, :]
            for j in range(plan.ctx):
                store(j, lanes, scaled[j * ROWS : (j + 1) * ROWS].astype(jnp.bfloat16))

    def keep_key(j, lanes, value):
        pbuf[j, 0, :, lanes] = value

    def keep_value(j, lanes, value):
        pbuf[j, 1, :, lanes] = value

    def keep_query(j, lanes, value):
        qbuf[j, :, lanes] = value

    def swap(src, dst, sem):
        order = [o for o in range(1, plan.ctx) if o % 2] + [o for o in range(2, plan.ctx, 2)]

        def copy(o, slot):
            return copy_to(src.at[ctx ^ o], dst.at[slot], sem.at[0, o], sem.at[1, o], {"ctx": ctx ^ o})

        for o in order:
            copy(o, ctx).start()
        dst[ctx] = src[ctx]

        def arrive():
            for o in order:
                copy(o, ctx ^ o).wait_recv()

        def drain():
            for o in order:
                copy(o, ctx).wait_send()

        return arrive, drain

    project(1, keep_key)
    project(2, keep_value)
    arrive_gate, drain_gate = swap(pbuf, rbuf, asem)
    project(0, keep_query)
    arrive_query, drain_query = swap(qbuf, qrecv, qsem)

    @pl.loop(1, plane)
    def _(o):
        plane_copy(o).wait_send()

    @pl.loop(1, ring)
    def _(o):
        ring_copy(o).wait_send()

    drain1()
    arrive_gate()

    for j in range(plan.ctx):
        for s in range(2):
            seq[s + 1, :, LANES + j * tokens : LANES + (j + 1) * tokens] = rbuf[j, s].astype(jnp.float32)

    def smooth(s):
        taps = [tapb[3 * s + k, pl.ds(ctx * ROWS, ROWS), :][:, 0:1] for k in range(3)]
        full = seq[s]
        total = taps[0] * full + taps[1] * pltpu.roll(full, 1, 1)
        total = total + taps[2] * pltpu.roll(full, 2, 1)
        return total[:, LANES:]

    gated = (smooth(1) * smooth(2)).astype(jnp.bfloat16).astype(jnp.float32)
    blocks = plan.blocks
    for b in range(blocks):
        gseq[pl.ds(blocks + b, ROWS, stride=2 * blocks), :] = gated[:, b * LANES : (b + 1) * LANES]

    @pl.loop(0, ROWS, unroll=4)
    def _(c):
        base = c * 2 * blocks + blocks
        lhs = jnp.concatenate(
            [gseq[pl.ds(base - d, blocks), :].astype(jnp.bfloat16) for d in range(blocks)], axis=1
        )
        rhs = tmat[pl.ds(c * blocks, blocks)].reshape(blocks * LANES, LANES)
        fseq[pl.ds(c * blocks, blocks), :] = jnp.dot(lhs, rhs, preferred_element_type=jnp.float32)

    arrive_query()
    for j in range(plan.ctx):
        seq[0, :, LANES + j * tokens : LANES + (j + 1) * tokens] = qrecv[j].astype(jnp.float32)
    query = smooth(0)
    direct = skipb[pl.ds(ctx * ROWS, ROWS), :]
    for b in range(blocks):
        lanes = slice(b * LANES, (b + 1) * LANES)
        value = query[:, lanes] * (fseq[pl.ds(b, ROWS, stride=blocks), :] + direct * gated[:, lanes])
        j, k = b // plan.token_tiles, b % plan.token_tiles
        mbuf[j, :, k * LANES : (k + 1) * LANES] = value.astype(jnp.bfloat16)

    arrive_mixed, drain_mixed = swap(mbuf, mrecv, bsem)
    drain_gate()
    drain_query()
    arrive_mixed()
    mixg[me] = mrecv[...].astype(jnp.float32).reshape(rows, tokens).astype(jnp.bfloat16)

    drain4 = gather(mixg, zsem2, ysem2, lastsem2, csem2, multiply_out, [])
    out[...] = acc2[...].astype(jnp.bfloat16)
    drain_mixed()
    drain4()


def shards(fsdp, ctx, activations, norm_gain, w_in, w_short, long_filter, skip_gain, w_out):
    rows, tokens = activations.shape
    long_len = long_filter.shape[1]
    plan = Plan(fsdp, ctx, rows, tokens, long_len)
    groups = rows // ROWS
    features = fsdp * rows
    bf16, f32 = jnp.bfloat16, jnp.float32
    dma = pltpu.SemaphoreType.DMA
    anywhere = pl.BlockSpec(memory_space=pl.ANY)
    here = pl.BlockSpec(memory_space=pltpu.VMEM)
    gather_sems = [
        dma((2, max(plan.line, 2))),
        dma((2, plan.ring, plan.line)),
        dma((2, plan.ring, max(plan.line, 2))),
        dma((2, plan.ring, plan.line)),
    ]
    scratch = [
        pltpu.VMEM((fsdp, rows, tokens), bf16),
        pltpu.VMEM((fsdp, rows, tokens), bf16),
        pltpu.VMEM((3, rows, features), bf16),
        pltpu.VMEM((rows, features), bf16),
        pltpu.VMEM((rows, tokens), bf16),
        pltpu.VMEM((ROWS, long_len), bf16),
        pltpu.VMEM((ROWS * plan.blocks, LANES), f32),
        pltpu.VMEM((ROWS * plan.blocks, LANES, LANES), bf16),
        pltpu.VMEM((3 * rows, tokens), f32),
        pltpu.VMEM((rows, tokens), f32),
        pltpu.VMEM((plan.plane, ROWS, LANES), f32),
        pltpu.VMEM((plan.ring, ROWS, LANES), f32),
        pltpu.VMEM((ROWS, LANES), f32),
        pltpu.VMEM((ctx, 2, ROWS, tokens), bf16),
        pltpu.VMEM((ctx, 2, ROWS, tokens), bf16),
        pltpu.VMEM((ctx, ROWS, tokens), bf16),
        pltpu.VMEM((ctx, ROWS, tokens), bf16),
        pltpu.VMEM((ctx, ROWS, tokens), bf16),
        pltpu.VMEM((ctx, ROWS, tokens), bf16),
        pltpu.VMEM((3, ROWS, LANES + long_len), f32),
        pltpu.VMEM((ROWS * 2 * plan.blocks, LANES), f32),
        pltpu.VMEM((ROWS * plan.blocks, LANES), f32),
        pltpu.VMEM((rows, LANES), f32),
        pltpu.VMEM((9, rows, LANES), f32),
        dma((4,)),
        dma((2, plan.plane)),
        dma((2, plan.ring)),
        *gather_sems,
        *gather_sems,
        dma((2, ctx)),
        dma((2, ctx)),
        dma((2, ctx)),
    ]
    return pl.pallas_call(
        functools.partial(kernel, plan),
        out_shape=jax.ShapeDtypeStruct((rows, tokens), bf16),
        in_specs=[anywhere, here, anywhere, here, anywhere, here, anywhere],
        out_specs=here,
        scratch_shapes=scratch,
        compiler_params=pltpu.CompilerParams(
            collective_id=0, has_side_effects=True, vmem_limit_bytes=56 * 1024 * 1024
        ),
        name="mixer",
    )(
        activations,
        norm_gain.reshape(1, rows),
        w_in,
        jnp.transpose(w_short, (0, 2, 1)),
        long_filter.reshape(groups, ROWS, long_len),
        skip_gain.reshape(1, rows),
        w_out,
    )


def solution(mesh):
    placed = (
        P("fsdp", "ctx"),
        P("fsdp"),
        P(None, "fsdp", None),
        P(None, "fsdp", None),
        P("fsdp", None),
        P("fsdp"),
        P("fsdp", None),
    )
    body = functools.partial(shards, mesh.shape["fsdp"], mesh.shape["ctx"])
    return jax.shard_map(body, mesh=mesh, in_specs=placed, out_specs=P("fsdp", "ctx"), check_vma=False)
```
